32 devices in a mesh: dom: 4 (over y, x), head: 8 (over z, core).
Axes of the slice: x: 2, y: 2, z: 4, core: 2. Of those that a mesh axis runs over, the one named last changes fastest.
Arguments:
- tokens: bfloat16 [24, 64, 8192], P(None, 'dom', 'head'), may hold values from -6 to 6
- parents: int32 [64], replicated, may hold values from 0 to 63, as said below
- recurrent_state: float32 [64, 128, 64, 256], P('dom', 'head'), may hold values from -6 to 6
- value_history: float32 [64, 3, 8192], P('dom', None, 'head'), may hold values from -6 to 6
- mixing_history: float32 [64, 3, 2048], P('dom', None, 'head'), may hold values from -6 to 6
- input_gain: float32 [8192], P('head'), may hold values from 0.5 to 1.5
- gate_value_weight: bfloat16 [8192, 2, 8192], P(None, None, 'head'), may hold values from -0.0625 to 0.0625
- mixing_weight: bfloat16 [8192, 2048], P(None, 'head'), may hold values from -0.0625 to 0.0625
- step_weight: bfloat16 [8192, 128], P(None, 'head'), may hold values from -0.0625 to 0.0625
- value_kernel: float32 [4, 8192], P(None, 'head'), may hold values from -3 to 3
- value_offset: float32 [8192], P('head'), may hold values from -0.5 to 0.5
- mixing_kernel: float32 [4, 2048], P(None, 'head'), may hold values from -3 to 3
- mixing_offset: float32 [2048], P('head'), may hold values from -0.5 to 0.5
- step_offset: float32 [128], P('head'), may hold values from -4 to 0
- decay_log: float32 [128], P('head'), may hold values from -2 to 1.5
- skip_gain: float32 [128], P('head'), may hold values from 0.5 to 1.5
- output_gain: float32 [8192], P('head'), may hold values from 0.5 to 1.5
- output_weight: bfloat16 [8192, 8192], P('head'), may hold values from -0.0625 to 0.0625
Outputs:
- mixed: bfloat16 [24, 64, 8192], P(None, 'dom', 'head')
The draws below stay inside these ranges and needn't reach their ends.
Inputs may be any that keep to these rules, and one draw needn't show every extreme that they name: parents comes from systematic resampling: it never falls with i, and offspring counts are very uneven, so that a particle's parent may sit several blocks of 16 particles away.
All inputs are finite; a program needn't handle non-finite values.
Results may differ from the reference program's by a relative error of at most 0.023.
Values may be sent and summed in bfloat16 or wider, within the bound.
No kernel may reach another device: no remote copies, remote signals or barrier semaphores. Data moves between devices by JAX's collectives and lax.ppermute only.
A program may use at most 256 MiB of HBM per device.

```python
import jax
import jax.numpy as jnp
from jax import lax

D = 8192
HEADS = 128
GROUPS = 4
P_SIZE = 64
N = 256
K = 4
STEPS = 24
PARTICLES = 64


def draw_parents(key, part):
    count = PARTICLES
    key_base, key_place, key_offset = jax.random.split(key, 3)
    base_weight = jax.random.randint(key_base, (count,), 1, 64)
    quarter = count // 4
    hot_start = jax.random.randint(key_place, (), 0, count - quarter + 1)
    position = jnp.arange(count, dtype=jnp.int32)
    inside = (position >= hot_start) & (position < hot_start + quarter)
    weights = base_weight * jnp.where(inside, 16, 1)
    cumulative = jnp.cumsum(weights).astype(jnp.int32)
    grand_total = cumulative[count - 1]
    offset = jax.random.randint(key_offset, (), 0, grand_total)
    target = offset + position * grand_total
    below = cumulative[None, :] * count <= target[:, None]
    chosen = jnp.sum(below.astype(jnp.int32), axis=1).astype(jnp.int32)
    chosen = chosen.at[0].set(0)
    chosen = chosen.at[count - 1].set(count - 1)
    return chosen


def levels(key, extent, shards, smallest, high):
    def one(dim, parts):
        draws = jax.random.uniform(jax.random.fold_in(jax.random.fold_in(key, 6), dim), (parts,), jnp.float32, smallest / len(shards), high / len(shards))
        return jnp.repeat(jnp.exp(draws), extent[dim] // parts).reshape((-1,) + (1,) * (len(extent) - dim - 1))

    gain = one(*shards[0])
    for cut in shards[1:]:
        gain = gain * one(*cut)
    return gain


def noise(own_key, extent, scale, reach, cuts=(), kind=jnp.bfloat16):
    array = scale * jax.random.normal(own_key, extent, jnp.float32)
    if cuts:
        array = array * levels(own_key, extent, cuts, -0.22, 0.18)
    return jnp.clip(array, -reach, reach).astype(kind)


def setup_inputs(seed: int = 0) -> dict:
    splits = jax.random.split(jax.random.key(seed), 19)
    return {
        "tokens": noise(splits[0], (STEPS, PARTICLES, D), 1.0, 6.0, ((1, 4), (2, 8))),
        "parents": draw_parents(jax.random.fold_in(splits[18], 71), 0),
        "recurrent_state": noise(splits[2], (PARTICLES, HEADS, P_SIZE, N), 1.0, 6.0, ((0, 4), (1, 8)), jnp.float32),
        "value_history": noise(splits[3], (PARTICLES, K - 1, HEADS * P_SIZE), 1.0, 6.0, ((0, 4), (2, 8)), jnp.float32),
        "mixing_history": noise(splits[4], (PARTICLES, K - 1, 2 * GROUPS * N), 1.0, 6.0, ((0, 4), (2, 8)), jnp.float32),
        "input_gain": jnp.clip(1.0 + 0.1 * jax.random.normal(splits[5], (D,), jnp.float32), 0.5, 1.5),
        "gate_value_weight": noise(splits[6], (D, 2, HEADS * P_SIZE), D ** -0.5, 0.0625, ((2, 8),)),
        "mixing_weight": noise(splits[7], (D, 2 * GROUPS * N), D ** -0.5, 0.0625, ((1, 8),)),
        "step_weight": noise(splits[8], (D, HEADS), D ** -0.5, 0.0625, ((1, 8),)),
        "value_kernel": noise(splits[9], (K, HEADS * P_SIZE), K ** -0.5, 3.0, ((1, 8),), jnp.float32),
        "value_offset": jnp.clip(jax.random.uniform(splits[10], (HEADS * P_SIZE,), jnp.float32, -0.5, 0.5) * levels(splits[10], (HEADS * P_SIZE,), ((0, 8),), -0.4, 0.0), -0.5, 0.5),
        "mixing_kernel": noise(splits[11], (K, 2 * GROUPS * N), K ** -0.5, 3.0, ((1, 8),), jnp.float32),
        "mixing_offset": jnp.clip(jax.random.uniform(splits[12], (2 * GROUPS * N,), jnp.float32, -0.5, 0.5) * levels(splits[12], (2 * GROUPS * N,), ((0, 8),), -0.4, 0.0), -0.5, 0.5),
        "step_offset": jnp.clip(-4.0 + 4.0 * jax.random.uniform(splits[13], (HEADS,), jnp.float32) ** levels(splits[13], (HEADS,), ((0, 8),), -0.2, 0.2), -4.0, 0.0),
        "decay_log": jnp.clip(-2.0 + 3.5 * jax.random.uniform(splits[14], (HEADS,), jnp.float32) ** levels(splits[14], (HEADS,), ((0, 8),), -0.2, 0.2), -2.0, 1.5),
        "skip_gain": jnp.clip(0.5 + 1.0 * jax.random.uniform(splits[15], (HEADS,), jnp.float32) ** levels(splits[15], (HEADS,), ((0, 8),), -0.2, 0.2), 0.5, 1.5),
        "output_gain": jnp.clip(1.0 + 0.1 * jax.random.normal(splits[16], (HEADS * P_SIZE,), jnp.float32), 0.5, 1.5),
        "output_weight": noise(splits[17], (HEADS * P_SIZE, D), (HEADS * P_SIZE) ** -0.5, 0.0625, ((0, 8),)),
    }


def causal_conv(previous, current, kernel, shift_bias):
    window = jnp.concatenate([jnp.moveaxis(previous, 1, 0), current], axis=0)
    length = current.shape[0]
    summed = jnp.zeros_like(current)
    for tap_index in range(kernel.shape[0]):
        summed = summed + kernel[tap_index] * window[tap_index:tap_index + length]
    return jax.nn.silu(summed + shift_bias)

def reference(tokens, parents, recurrent_state, value_history, mixing_history, input_gain, gate_value_weight, mixing_weight, step_weight, value_kernel, value_offset, mixing_kernel, mixing_offset, step_offset, decay_log, skip_gain, output_gain, output_weight):
    channels = HEADS * P_SIZE
    heads_group = HEADS // GROUPS
    flat_tokens = tokens.astype(jnp.float32).reshape(STEPS * PARTICLES, D)
    normed = (flat_tokens * lax.rsqrt(lax.optimization_barrier(jnp.mean(flat_tokens * flat_tokens, axis=-1, keepdims=True)) + 1e-05) * input_gain).astype(jnp.bfloat16)
    gate_value = jnp.dot(normed, gate_value_weight.reshape(D, 2 * channels), preferred_element_type=jnp.float32).reshape(STEPS, PARTICLES, 2, channels)
    mixing_raw = jnp.dot(normed, mixing_weight, preferred_element_type=jnp.float32).reshape(STEPS, PARTICLES, 2 * GROUPS * N)
    step_raw = jnp.dot(normed, step_weight, preferred_element_type=jnp.float32).reshape(STEPS, PARTICLES, HEADS)
    value_prev = jnp.take(value_history, parents, axis=0)
    mixing_prev = jnp.take(mixing_history, parents, axis=0)
    value_act = causal_conv(value_prev, gate_value[:, :, 1], value_kernel, value_offset).reshape(STEPS, PARTICLES, HEADS, P_SIZE)
    mixing_act = causal_conv(mixing_prev, mixing_raw, mixing_kernel, mixing_offset)
    step_size = jax.nn.softplus(step_raw + step_offset)
    decay = jnp.exp(-step_size * jnp.exp(decay_log))

    def per_group(group_index):
        first_head = group_index * heads_group
        start_state = jnp.take(lax.dynamic_slice_in_dim(recurrent_state, first_head, heads_group, 1), parents, axis=0)
        input_mix = lax.dynamic_slice_in_dim(mixing_act, group_index * N, N, 2)
        output_mix = lax.dynamic_slice_in_dim(mixing_act, (GROUPS + group_index) * N, N, 2)
        values = lax.dynamic_slice_in_dim(value_act, first_head, heads_group, 2)
        sizes = lax.dynamic_slice_in_dim(step_size, first_head, heads_group, 2)
        decays = lax.dynamic_slice_in_dim(decay, first_head, heads_group, 2)
        skips = lax.dynamic_slice_in_dim(skip_gain, first_head, heads_group, 0)

        def advance(state_now, inputs):
            value_now, input_now, output_now, size_now, decay_now = inputs
            state_now = decay_now[:, :, None, None] * state_now + (size_now[:, :, None] * value_now)[..., None] * input_now[:, None, None, :]
            read_out = jnp.einsum('bhpn,bn->bhp', state_now, output_now, precision=lax.Precision.HIGHEST)
            return (state_now, read_out + skips[:, None] * value_now)
        unused_state, reads = lax.scan(advance, start_state, (values, input_mix, output_mix, sizes, decays))
        return reads
    reads = lax.map(per_group, jnp.arange(GROUPS, dtype=jnp.int32))
    read_all = jnp.moveaxis(reads, 0, 2).reshape(STEPS, PARTICLES, GROUPS, heads_group * P_SIZE)
    gated = read_all * jax.nn.silu(gate_value[:, :, 0].reshape(STEPS, PARTICLES, GROUPS, heads_group * P_SIZE))
    square_mean = lax.optimization_barrier(jnp.sum(gated * gated, axis=-1, keepdims=True)) / (heads_group * P_SIZE)
    scaled = ((gated * lax.rsqrt(square_mean + 1e-05)).reshape(STEPS * PARTICLES, channels) * output_gain).astype(jnp.bfloat16)
    mixed = jnp.dot(scaled, output_weight, preferred_element_type=jnp.float32).astype(jnp.bfloat16)
    return mixed.reshape(STEPS, PARTICLES, D)
```

```python
import functools

import jax
import jax.numpy as jnp
from jax import lax
from jax.experimental import pallas as pl
from jax.experimental.pallas import tpu as pltpu
from jax.sharding import PartitionSpec as P

GROUPS = 4
CHUNKS = 2
LANES = 128
EXTRA = 8
HIGH = lax.Precision.HIGHEST
F32 = jnp.float32
BF16 = jnp.bfloat16


def params(mib=48):
    return pltpu.CompilerParams(vmem_limit_bytes=mib << 20)


def cost(flops, nbytes):
    return pl.CostEstimate(flops=flops, bytes_accessed=nbytes, transcendentals=0)


def whole_spec(shape):
    return pl.BlockSpec(shape, lambda *_: (0,) * len(shape))


def silu(v):
    return v / (1.0 + jnp.exp(-v))


def prepare_kernel(tok_ref, gain_ref, out_ref):
    steps, particles, width = tok_ref.shape
    count = out_ref.shape[0]
    each = particles // count
    rows = steps * each
    padded = -(-rows // LANES) * LANES
    for k in range(count):
        x = tok_ref[...].astype(F32)[:, k * each : (k + 1) * each, :].reshape(rows, width)
        out_ref[k, :rows, :] = (x * gain_ref[...]).astype(BF16)
        sq = jnp.concatenate([x * x, jnp.zeros((padded - rows, width), F32)], axis=0)
        total = lax.dot_general(
            jnp.ones((EXTRA, width), F32),
            sq,
            (((1,), (1,)), ((), ())),
            precision=HIGH,
            preferred_element_type=F32,
        )
        high = total.astype(BF16).astype(F32)
        which = lax.broadcasted_iota(jnp.int32, total.shape, 0)
        both = jnp.where(which == 0, high, jnp.where(which == 1, total - high, 0.0))
        if padded < width:
            both = jnp.concatenate([both, jnp.zeros((EXTRA, width - padded), F32)], axis=1)
        out_ref[k, rows:, :] = both.astype(BF16)


def prepare(tokens, gain):
    steps, particles, width = tokens.shape
    rows = steps * particles // CHUNKS
    return pl.pallas_call(
        prepare_kernel,
        out_shape=jax.ShapeDtypeStruct((CHUNKS, rows + EXTRA, width), BF16),
        compiler_params=params(),
        name="prepare",
    )(tokens, gain.reshape(1, -1))


def split_kernel(w_ref, o_ref):
    depth, _, width = w_ref.shape
    half = min(LANES, depth)
    row = lax.broadcasted_iota(jnp.int32, (2 * half, 2 * half), 0)
    col = lax.broadcasted_iota(jnp.int32, (2 * half, 2 * half), 1)
    source = jnp.where(row < half, 2 * row, 2 * (row - half) + 1)
    move = (source == col).astype(F32).astype(BF16)
    for i in range(depth // half):
        part = w_ref[i * half : (i + 1) * half].reshape(2 * half, width)
        moved = jnp.dot(move, part, preferred_element_type=F32).astype(BF16)
        o_ref[0, i * half : (i + 1) * half, :] = moved[:half]
        o_ref[1, i * half : (i + 1) * half, :] = moved[half:]


def split_weights(w):
    depth, _, width = w.shape
    block = min(1024, depth)
    return pl.pallas_call(
        split_kernel,
        grid=(depth // block,),
        in_specs=[pl.BlockSpec((block, 2, width), lambda k: (k, 0, 0))],
        out_specs=pl.BlockSpec((2, block, width), lambda k: (0, k, 0)),
        out_shape=jax.ShapeDtypeStruct((2, depth, width), BF16),
        compiler_params=params(),
        cost_estimate=cost(4 * depth * width * 256, 8 * depth * width),
        name="split_weights",
    )(w)


def fetch_slot(step, pick, slots, refs, xs_ref):
    for k, (first, second) in enumerate(slots):

        @pl.when(step == k)
        def _():
            if second is None:
                xs_ref[...] = refs[first][...]
            else:

                @pl.when(pick[k] == 1)
                def _():
                    xs_ref[...] = refs[first][...]

                @pl.when(pick[k] != 1)
                def _():
                    xs_ref[...] = refs[second][...]


def narrow_kernel(slots, count, idx, pick, *refs):
    xs, (wm_ref, ws_ref, mix_ref, step_ref, extra_ref, xs_ref) = refs[:count], refs[count:]
    i = pl.program_id(0)
    fetch_slot(i, pick, slots, xs, xs_ref)
    rows = mix_ref.shape[0]

    @pl.when(i == 0)
    def _():
        mix_ref[...] = jnp.zeros_like(mix_ref)
        step_ref[...] = jnp.zeros_like(step_ref)
        extra_ref[...] = jnp.zeros_like(extra_ref)

    x = xs_ref[:rows, :]
    mix_ref[...] += jnp.dot(x, wm_ref[...], preferred_element_type=F32)
    step_ref[...] += lax.dot_general(
        x, ws_ref[...], (((1,), (1,)), ((), ())), preferred_element_type=F32
    )
    extra_ref[...] += xs_ref[rows:, :].astype(F32)


def wide_kernel(slots, count, idx, pick, *refs):
    xs, (w_ref, gate_ref, value_ref, xs_ref) = refs[:count], refs[count:]
    i = pl.program_id(0)
    fetch_slot(i, pick, slots, xs, xs_ref)
    rows = gate_ref.shape[0]

    @pl.when(i == 0)
    def _():
        gate_ref[...] = jnp.zeros_like(gate_ref)
        value_ref[...] = jnp.zeros_like(value_ref)

    x = xs_ref[:rows, :]
    value_ref[...] += jnp.dot(x, w_ref[1], preferred_element_type=F32)
    gate_ref[...] += jnp.dot(x, w_ref[0], preferred_element_type=F32)


def project_narrow(slots, idx, pick, arrays, mixing_weight, step_weight_t):
    ext, width = arrays[0].shape
    rows = ext - EXTRA
    columns, heads = mixing_weight.shape[1], step_weight_t.shape[0]
    depth = mixing_weight.shape[0]
    grid_spec = pltpu.PrefetchScalarGridSpec(
        num_scalar_prefetch=2,
        grid=(len(slots),),
        in_specs=[whole_spec((ext, width))] * len(arrays)
        + [
            pl.BlockSpec((width, columns), lambda i, idx, pick: (idx[i], 0)),
            pl.BlockSpec((heads, width), lambda i, idx, pick: (0, idx[i])),
        ],
        out_specs=[
            whole_spec((rows, columns)),
            whole_spec((rows, heads)),
            whole_spec((EXTRA, width)),
        ],
        scratch_shapes=[pltpu.VMEM((ext, width), BF16)],
    )
    return pl.pallas_call(
        functools.partial(narrow_kernel, slots, len(arrays)),
        grid_spec=grid_spec,
        out_shape=[
            jax.ShapeDtypeStruct((rows, columns), F32),
            jax.ShapeDtypeStruct((rows, heads), F32),
            jax.ShapeDtypeStruct((EXTRA, width), F32),
        ],
        compiler_params=params(),
        cost_estimate=cost(2 * rows * depth * (columns + heads), 2 * depth * (columns + heads)),
        name="project_narrow",
    )(idx, pick, *arrays, mixing_weight, step_weight_t)


def project_wide(slots, idx, pick, arrays, weights):
    ext, width = arrays[0].shape
    rows = ext - EXTRA
    _, depth, channels = weights.shape
    grid_spec = pltpu.PrefetchScalarGridSpec(
        num_scalar_prefetch=2,
        grid=(len(slots),),
        in_specs=[whole_spec((ext, width))] * len(arrays)
        + [pl.BlockSpec((2, width, channels), lambda i, idx, pick: (0, idx[i], 0))],
        out_specs=[whole_spec((rows, channels))] * 2,
        scratch_shapes=[pltpu.VMEM((ext, width), BF16)],
    )
    return pl.pallas_call(
        functools.partial(wide_kernel, slots, len(arrays)),
        grid_spec=grid_spec,
        out_shape=[jax.ShapeDtypeStruct((rows, channels), F32)] * 2,
        compiler_params=params(),
        cost_estimate=cost(4 * rows * depth * channels, 4 * depth * channels),
        name="project_wide",
    )(idx, pick, *arrays, weights)


TOGETHER = 4


def owner_kernel(low, high, c_ref, s_ref, o_ref):
    p = pl.program_id(0)
    first, last = low[p], high[p]
    _, heads, head_width, state_width = s_ref.shape
    steps = c_ref.shape[1]
    channels = heads * head_width

    @pl.when(last > first)
    def _():
        state = s_ref[0].reshape(channels, state_width).astype(BF16)

        def some(g, carry):
            base = first + g * TOGETHER
            c = c_ref[pl.ds(base, TOGETHER)].astype(F32)
            c = c.reshape(TOGETHER * steps, state_width).astype(BF16)
            r = lax.dot_general(
                c, state, (((1,), (1,)), ((), ())), preferred_element_type=F32
            ).reshape(TOGETHER, steps, channels)
            for i in range(TOGETHER):

                @pl.when(base + i < last)
                def _():
                    o_ref[base + i] = r[i].astype(BF16)

            return carry

        lax.fori_loop(0, (last - first + TOGETHER - 1) // TOGETHER, some, 0)


def owner_reads(low, high, child_mix, state):
    children, steps, state_width = child_mix.shape
    particles, heads, head_width, _ = state.shape
    channels = heads * head_width
    grid_spec = pltpu.PrefetchScalarGridSpec(
        num_scalar_prefetch=2,
        grid=(particles,),
        in_specs=[
            whole_spec(child_mix.shape),
            pl.BlockSpec((1, heads, head_width, state_width), lambda p, *_: (p, 0, 0, 0)),
        ],
        out_specs=whole_spec((children, steps, channels)),
    )
    return pl.pallas_call(
        owner_kernel,
        grid_spec=grid_spec,
        out_shape=jax.ShapeDtypeStruct((children, steps, channels), BF16),
        compiler_params=params(),
        cost_estimate=cost(
            2 * children * steps * channels * state_width, 4 * particles * channels * state_width
        ),
        name="owner_reads",
    )(low, high, child_mix, state)


def local_kernel(
    v_ref, rs_ref, hist_ref, tap_ref, bias_ref, b_ref, c_ref, step_ref, decay_ref, skip_ref,
    y_ref, cum_ref, dot_ref, head_width,
):
    steps, each, channels = v_ref.shape
    taps = tap_ref.shape[0]
    for t in range(steps):
        c = c_ref[t].astype(F32)
        for s in range(t + 1):
            product = jnp.sum(c * b_ref[s].astype(F32), axis=-1, keepdims=True)
            dot_ref[t * (t + 1) // 2 + s] = jnp.broadcast_to(product, (each, LANES))

    def tile(i, carry):
        at = pl.ds(pl.multiple_of(i * LANES, LANES), LANES)
        head = lax.broadcasted_iota(jnp.int32, (LANES, LANES), 0)
        lane = lax.broadcasted_iota(jnp.int32, (LANES, LANES), 1) + i * LANES
        spread = (lane // head_width == head).astype(F32)

        def expand(x):
            return jnp.dot(x, spread, precision=HIGH, preferred_element_type=F32)

        size = expand(step_ref[...]).reshape(steps, each, LANES)
        decay = expand(decay_ref[...]).reshape(steps, each, LANES)
        skip = expand(skip_ref[...])[0:1, :]
        seq = [hist_ref[k, :, at] for k in range(taps - 1)]
        seq += [v_ref[t, :, at] * rs_ref[t] for t in range(steps)]
        tap = tap_ref[:, at]
        bias = bias_ref[:, at]
        held = []
        cum = None
        for t in range(steps):
            total = bias
            for k in range(taps):
                total = total + tap[k : k + 1, :] * seq[t + k]
            value = silu(total)
            d = decay[t]
            cum = d if t == 0 else cum * d
            cum_ref[t, :, at] = cum
            held = [h * d for h in held] + [size[t] * value]
            y = skip * value
            for s in range(t + 1):
                y = y + dot_ref[t * (t + 1) // 2 + s] * held[s]
            y_ref[t, :, at] = y
        return carry

    lax.fori_loop(0, channels // LANES, tile, 0)


def local_reads(value, rs, history, taps, bias, b, c, size, decay, skip, head_width):
    steps, each, channels = value.shape
    return pl.pallas_call(
        functools.partial(local_kernel_entry, head_width),
        out_shape=[jax.ShapeDtypeStruct((steps, each, channels), F32)] * 2,
        scratch_shapes=[pltpu.VMEM((steps * (steps + 1) // 2, each, LANES), F32)],
        compiler_params=params(),
        cost_estimate=cost(steps * steps * each * channels * 16, 12 * steps * each * channels),
        name="local_reads",
    )(value, rs, history, taps, bias, b, c, size, decay, skip)


def local_kernel_entry(head_width, *refs):
    local_kernel(*refs, head_width=head_width)


def out_kernel(idx, x_ref, w_ref, o_ref):
    o_ref[0] = jnp.dot(x_ref[...], w_ref[...], preferred_element_type=F32).astype(BF16)


def project_out(idx, x, weight, width):
    rows, channels = x.shape
    count = idx.shape[0]
    grid_spec = pltpu.PrefetchScalarGridSpec(
        num_scalar_prefetch=1,
        grid=(count,),
        in_specs=[
            whole_spec((rows, channels)),
            pl.BlockSpec((channels, width), lambda i, idx: (0, idx[i])),
        ],
        out_specs=pl.BlockSpec((1, rows, width), lambda i, idx: (i, 0, 0)),
    )
    return pl.pallas_call(
        out_kernel,
        grid_spec=grid_spec,
        out_shape=jax.ShapeDtypeStruct((count, rows, width), BF16),
        compiler_params=params(),
        cost_estimate=cost(2 * rows * channels * count * width, 2 * channels * count * width),
        name="project_out",
    )(idx, x, weight)


def conv(previous, current, kernel, shift_bias):
    window = jnp.concatenate([previous, current], axis=0)
    length = current.shape[0]
    summed = jnp.zeros_like(current)
    for k in range(kernel.shape[0]):
        summed = summed + kernel[k] * window[k : k + length]
    return silu(summed + shift_bias)


def pad_lanes(x):
    return jnp.pad(x, ((0, 0), (0, LANES - x.shape[1])))


def body(
    tokens,
    parents,
    recurrent_state,
    value_history,
    mixing_history,
    input_gain,
    gate_value_weight,
    mixing_weight,
    step_weight,
    value_kernel,
    value_offset,
    mixing_kernel,
    mixing_offset,
    step_offset,
    decay_log,
    skip_gain,
    output_gain,
    output_weight,
):
    steps, particles, width = tokens.shape
    _, heads, head_width, state_width = recurrent_state.shape
    channels = heads * head_width
    each = particles // CHUNKS
    rows = steps * each
    doms = lax.axis_size("dom")
    dom = lax.axis_index("dom")
    ranks = lax.axis_size("head")
    rank = lax.axis_index("head")
    pairs = ranks // 2
    z, core = rank // 2, rank % 2
    features = width * ranks

    def swap(x):
        return lax.ppermute(x, "head", [(i, i ^ 1) for i in range(ranks)])

    def up(x, first, stop):
        return lax.ppermute(
            x, "head", [(2 * i + c, 2 * i + 2 + c) for i in range(first, stop) for c in (0, 1)]
        )

    def down(x, first, stop):
        return lax.ppermute(
            x, "head", [(2 * i + c, 2 * i - 2 + c) for i in range(first, stop) for c in (0, 1)]
        )

    def across(x, k):
        return lax.ppermute(x, "dom", [(i, i ^ k) for i in range(doms)])

    prepared = prepare(tokens, input_gain)

    slots, indices, picks = [(0, None), (1, None)], [rank, rank ^ 1], [1, 1]
    for j in range(1, pairs):
        source = (z + j) % pairs
        pick = (z + j < pairs).astype(jnp.int32)
        at = 2 + 4 * (j - 1)
        back = 2 + 4 * (pairs - j - 1)
        slots += [(at, back + 2), (at + 1, back + 3)]
        indices += [2 * source + core, 2 * source + 1 - core]
        picks += [pick, pick]
    idx = jnp.stack([jnp.asarray(v, jnp.int32) for v in indices])
    pick = jnp.stack([jnp.asarray(v, jnp.int32) for v in picks])

    def gather(own):
        arrays = [own, swap(own)]
        above, below = own, own
        for s in range(1, pairs):
            above = down(above, 1, pairs - s + 1)
            below = up(below, s - 1, pairs - 1)
            arrays += [above, swap(above), below, swap(below)]
        return arrays

    gathered = [gather(prepared[k]) for k in range(CHUNKS)]

    history = jnp.concatenate(
        [jnp.moveaxis(value_history, 1, 0), jnp.moveaxis(mixing_history, 1, 0)], axis=2
    ).astype(BF16)
    history_all = jnp.concatenate([history] + [across(history, k) for k in range(1, doms)], axis=1)
    first_child = dom * particles
    own_parents = lax.dynamic_slice_in_dim(parents, first_child, particles)
    held_at = ((own_parents // particles) ^ dom) * particles + own_parents % particles
    chosen = (held_at[:, None] == jnp.arange(doms * particles)[None, :]).astype(BF16)
    inherited = jnp.einsum("cp,tpw->tcw", chosen, history_all, preferred_element_type=F32)

    weights = split_weights(gate_value_weight)
    step_weight_t = step_weight.T

    per_group = ranks // GROUPS
    group = rank // per_group
    columns = mixing_weight.shape[1]

    def finish_mixing(k):
        part = slice(k * each, (k + 1) * each)
        mix_raw, step_raw, extra = project_narrow(
            slots, idx, pick, gathered[k], mixing_weight, step_weight_t
        )
        squares = (extra[0] + extra[1])[:rows].reshape(steps, each, 1)
        rs = lax.rsqrt(squares / features + 1e-05)
        mixing = conv(
            inherited[:, part, channels:],
            mix_raw.reshape(steps, each, columns) * rs,
            mixing_kernel,
            mixing_offset,
        ).astype(BF16)
        if columns == state_width and per_group == 2:
            moves = [(g, 2 * g) for g in range(GROUPS)]
            moves += [(GROUPS + g, 2 * g + 1) for g in range(GROUPS)]
            mine = lax.ppermute(mixing, "head", moves)
            other = swap(mine)
            b = jnp.where(core == 0, mine, other)
            c = jnp.where(core == 0, other, mine)
        else:
            every = lax.all_gather(mixing, "head", axis=2, tiled=True)
            b = lax.dynamic_slice_in_dim(every, group * state_width, state_width, 2)
            c = lax.dynamic_slice_in_dim(every, (GROUPS + group) * state_width, state_width, 2)
        size = jax.nn.softplus(
            step_raw.reshape(steps, each, heads) * rs + step_offset
        ).reshape(rows, heads)
        decay = jnp.exp(-size * jnp.exp(decay_log))
        return rs, b, c, size, decay

    def read_states(k, c):
        c_child = jnp.moveaxis(c, 1, 0)
        slabs = [c_child] + [across(c_child, j) for j in range(1, doms)]
        stacked = jnp.stack(slabs)
        order = jnp.arange(doms) ^ dom
        by_dom = jnp.stack([lax.dynamic_index_in_dim(stacked, order[d], 0, False) for d in range(doms)])
        child_mix = by_dom.reshape(doms * each, steps, state_width)
        child_mix = jnp.pad(child_mix, ((0, TOGETHER), (0, 0), (0, 0)))
        local = parents.reshape(doms, particles)[:, k * each : (k + 1) * each].reshape(-1) - first_child
        held = jnp.arange(particles)[:, None]
        low = jnp.sum((local[None, :] < held).astype(jnp.int32), axis=1)
        high = jnp.sum((local[None, :] <= held).astype(jnp.int32), axis=1)
        reads = owner_reads(low, high, child_mix, recurrent_state)
        reads = reads[: doms * each].reshape(doms, each, steps, channels)
        holder = lax.dynamic_slice_in_dim(own_parents, k * each, each) // particles
        result = lax.dynamic_index_in_dim(reads, dom, 0, False)
        for j in range(1, doms):
            received = across(lax.dynamic_index_in_dim(reads, dom ^ j, 0, False), j)
            result = jnp.where((holder == (dom ^ j))[:, None, None], received, result)
        return jnp.moveaxis(result, 1, 0)

    def finish(k, rs, b, c, size, decay, inherited_reads):
        part = slice(k * each, (k + 1) * each)
        gate, value = project_wide(slots, idx, pick, gathered[k], weights)
        rs_wide = jnp.broadcast_to(rs, (steps, each, LANES))
        y, cumulative = local_reads(
            value.reshape(steps, each, channels),
            rs_wide,
            inherited[:, part, :channels],
            value_kernel,
            value_offset.reshape(1, -1),
            b,
            c,
            pad_lanes(size),
            pad_lanes(decay),
            jnp.broadcast_to(pad_lanes(skip_gain.reshape(1, -1)), (8, LANES)),
            head_width,
        )
        read = cumulative * inherited_reads.astype(F32) + y
        gated = read * silu(gate.reshape(steps, each, channels) * rs)
        squares = jnp.sum(gated * gated, axis=2)
        total = squares
        for r in range(1, per_group):
            turn = [(i, i - i % per_group + (i + r) % per_group) for i in range(ranks)]
            total = total + lax.ppermute(squares, "head", turn)
        square_mean = total / (per_group * channels)
        return (
            (gated * lax.rsqrt(square_mean + 1e-05)[..., None] * output_gain)
            .reshape(rows, channels)
            .astype(BF16)
        )

    def scatter(scaled):
        blocks = jnp.arange(pairs, dtype=jnp.int32) * 2
        away = project_out(blocks + 1 - core, scaled, output_weight, width)
        here = project_out(blocks + core, scaled, output_weight, width)
        both = here.astype(F32) + swap(away).astype(F32)
        both = both.astype(BF16)

        def block(d):
            return lax.dynamic_index_in_dim(both, jnp.clip(d, 0, pairs - 1), 0, False).astype(F32)

        above = below = None
        for s in range(1, pairs):
            to_down = block(z - (pairs - s))
            to_up = block(z + (pairs - s))
            if s > 1:
                to_down, to_up = to_down + above.astype(F32), to_up + below.astype(F32)
            above = down(to_down.astype(BF16), pairs - s, pairs)
            below = up(to_up.astype(BF16), 0, s)
        result = block(z) + above.astype(F32) + below.astype(F32)
        return result.astype(BF16).reshape(steps, each, width)

    outputs = []
    for k in range(CHUNKS):
        rs, b, c, size, decay = finish_mixing(k)
        reads = read_states(k, c)
        scaled = finish(k, rs, b, c, size, decay, reads)
        outputs.append(scatter(scaled))
    return jnp.concatenate(outputs, axis=1)


def solution(mesh):
    return jax.shard_map(
        body,
        mesh=mesh,
        in_specs=(
            P(None, "dom", "head"),
            P(),
            P("dom", "head", None, None),
            P("dom", None, "head"),
            P("dom", None, "head"),
            P("head"),
            P(None, None, "head"),
            P(None, "head"),
            P(None, "head"),
            P(None, "head"),
            P("head"),
            P(None, "head"),
            P("head"),
            P("head"),
            P("head"),
            P("head"),
            P("head"),
            P("head", None),
        ),
        out_specs=P(None, "dom", "head"),
        check_vma=False,
    )
```

```python
import functools

import jax
import jax.numpy as jnp
from jax import lax
from jax.experimental import pallas as pl
from jax.experimental.pallas import tpu as pltpu
from jax.sharding import PartitionSpec as P


GROUPS = 4
CHUNKS = 2
LANES = 128
EXTRA = 8
PIECES = 4
HIGH = lax.Precision.HIGHEST
F32 = jnp.float32
BF16 = jnp.bfloat16


def params(mib=48):
    return pltpu.CompilerParams(vmem_limit_bytes=mib << 20)


def cost(flops, nbytes):
    return pl.CostEstimate(flops=flops, bytes_accessed=nbytes, transcendentals=0)


def whole_spec(shape):
    return pl.BlockSpec(shape, lambda *_: (0,) * len(shape))


def silu(v):
    return v / (1.0 + jnp.exp(-v))


def prepare_kernel(tok_ref, gain_ref, out_ref):
    steps, particles, width = tok_ref.shape
    count = out_ref.shape[0]
    each = particles // count
    rows = steps * each
    padded = -(-rows // LANES) * LANES
    for k in range(count):
        x = tok_ref[...].astype(F32)[:, k * each : (k + 1) * each, :].reshape(rows, width)
        out_ref[k, :rows, :] = (x * gain_ref[...]).astype(BF16)
        sq = jnp.concatenate([x * x, jnp.zeros((padded - rows, width), F32)], axis=0)
        total = lax.dot_general(
            jnp.ones((EXTRA, width), F32),
            sq,
            (((1,), (1,)), ((), ())),
            precision=HIGH,
            preferred_element_type=F32,
        )
        high = total.astype(BF16).astype(F32)
        which = lax.broadcasted_iota(jnp.int32, total.shape, 0)
        both = jnp.where(which == 0, high, jnp.where(which == 1, total - high, 0.0))
        if padded < width:
            both = jnp.concatenate([both, jnp.zeros((EXTRA, width - padded), F32)], axis=1)
        out_ref[k, rows:, :] = both.astype(BF16)


def prepare(tokens, gain):
    steps, particles, width = tokens.shape
    rows = steps * particles // CHUNKS
    return pl.pallas_call(
        prepare_kernel,
        out_shape=jax.ShapeDtypeStruct((CHUNKS, rows + EXTRA, width), BF16),
        compiler_params=params(),
        name="prepare",
    )(tokens, gain.reshape(1, -1))


def place(hop, pairs, i, rank):
    if hop == 0:
        return rank ^ i, True
    z, core = rank >> 1, rank & 1
    a, b = z + hop, z - hop
    has_a, has_b = a < pairs, b >= 0
    near = jnp.where(has_a, 2 * a + 1 - core, rank)
    far = jnp.where(has_b, 2 * b + core, near)
    from_above = jnp.where(has_a, 2 * a + (core ^ (i & 1)), far)
    from_below = jnp.where(has_b, 2 * b + (core ^ (i & 1)), near)
    return jnp.where(i < 2, from_above, from_below), jnp.where(i < 2, has_a, has_b)


def fetch_slot(valid, xs, x_ref):
    i = pl.program_id(0)
    for k in range(len(xs) // CHUNKS):

        @pl.when((i == k) & valid)
        def _():
            for chunk in range(CHUNKS):
                x_ref[chunk] = xs[CHUNKS * k + chunk][...]


def start_sums(sums, befores):
    @pl.when(pl.program_id(0) == 0)
    def _():
        for k, ref in enumerate(sums):
            ref[...] = befores[k][...] if befores else jnp.zeros_like(ref)


def narrow_kernel(count, with_sums, where, rank, *refs):
    valid = where(pl.program_id(0), rank[0])[1]
    xs, refs = refs[:count], refs[count:]
    wm_ref, ws_ref = refs[:2]
    refs = refs[2:]
    befores, refs = (refs[:4], refs[4:]) if with_sums else ((), refs)
    mix_ref, step_ref, extra_ref, all_ref, x_ref, sem = refs
    fetch_slot(valid, xs, x_ref)
    start_sums((mix_ref, step_ref, extra_ref), befores)
    rows = mix_ref.shape[1]

    @pl.when(valid)
    def _():
        for k in range(CHUNKS):
            x = x_ref[k, :rows, :]
            mix_ref[k] += jnp.dot(x, wm_ref[...], preferred_element_type=F32)
            step_ref[k] += lax.dot_general(
                x, ws_ref[...], (((1,), (1,)), ((), ())), preferred_element_type=F32
            )
            extra_ref[k] += x_ref[k, rows:, :].astype(F32)
        block = where(pl.program_id(0), rank[0])[0]
        copy = pltpu.make_async_copy(x_ref, all_ref.at[block], sem)
        copy.start()
        copy.wait()


def split_kernel(*refs):
    w_ref, o_ref = refs[0], refs[-1]
    depth, _, width = w_ref.shape
    half = min(LANES, depth)
    row = lax.broadcasted_iota(jnp.int32, (2 * half, 2 * half), 0)
    col = lax.broadcasted_iota(jnp.int32, (2 * half, 2 * half), 1)
    source = jnp.where(row < half, 2 * row, 2 * (row - half) + 1)
    move = (source == col).astype(F32).astype(BF16)
    for i in range(depth // half):
        part = w_ref[i * half : (i + 1) * half].reshape(2 * half, width)
        moved = jnp.dot(move, part, preferred_element_type=F32).astype(BF16)
        o_ref[0, i * half : (i + 1) * half, :] = moved[:half]
        o_ref[1, i * half : (i + 1) * half, :] = moved[half:]


def split_weights(w, piece, before):
    depth, _, width = w.shape
    block = depth // (2 * PIECES)
    return pl.pallas_call(
        split_kernel,
        grid=(2,),
        in_specs=[pl.BlockSpec((block, 2, width), lambda k: (2 * piece + k, 0, 0))]
        + [pl.BlockSpec(memory_space=pl.ANY)] * len(before),
        out_specs=pl.BlockSpec((2, block, width), lambda k: (0, 2 * piece + k, 0)),
        out_shape=jax.ShapeDtypeStruct((2, depth, width), BF16),
        input_output_aliases={1 + k: k for k in range(len(before))},
        compiler_params=params(),
        cost_estimate=cost(4 * block * width * 512, 16 * block * width),
        name="split_weights",
    )(w, *before)


def wide_kernel(x_ref, w_ref, o_ref):
    rows = o_ref.shape[1]
    depth = w_ref.shape[1]
    x = x_ref[0, :, :rows, :].astype(F32).reshape(CHUNKS * rows, depth).astype(BF16)
    y = jnp.dot(x, w_ref[0], preferred_element_type=F32).reshape(o_ref.shape)

    @pl.when(pl.program_id(0) == 0)
    def _():
        o_ref[...] = y

    @pl.when(pl.program_id(0) > 0)
    def _():
        o_ref[...] += y


def project_wide(which, features, weights):
    blocks, _, ext, width = features.shape
    rows = ext - EXTRA
    channels = weights.shape[2]
    shape = (CHUNKS, rows, channels)
    return pl.pallas_call(
        wide_kernel,
        grid=(blocks,),
        in_specs=[
            pl.BlockSpec((1, CHUNKS, ext, width), lambda i: (i, 0, 0, 0)),
            pl.BlockSpec((1, width, channels), lambda i: (which, i, 0)),
        ],
        out_specs=whole_spec(shape),
        out_shape=jax.ShapeDtypeStruct(shape, F32),
        compiler_params=params(),
        cost_estimate=cost(
            2 * CHUNKS * rows * width * blocks * channels, 2 * blocks * width * channels
        ),
        name="project_wide",
    )(features, weights)


def project_narrow(where, blocks, rank, arrays, mixing_weight, step_weight_t, sums):
    ext, width = arrays[0].shape
    rows = ext - EXTRA
    columns, heads = mixing_weight.shape[1], step_weight_t.shape[0]
    count = len(arrays) // CHUNKS
    shapes = [(CHUNKS, rows, columns), (CHUNKS, rows, heads), (CHUNKS, EXTRA, width)]
    anywhere = pl.BlockSpec(memory_space=pl.ANY)
    grid_spec = pltpu.PrefetchScalarGridSpec(
        num_scalar_prefetch=1,
        grid=(count,),
        in_specs=[whole_spec((ext, width))] * len(arrays)
        + [
            pl.BlockSpec((width, columns), lambda i, rank: (where(i, rank[0])[0], 0)),
            pl.BlockSpec((heads, width), lambda i, rank: (0, where(i, rank[0])[0])),
        ]
        + [whole_spec(x.shape) for x in sums[:3]]
        + [anywhere] * len(sums[3:]),
        out_specs=[whole_spec(x) for x in shapes] + [anywhere],
        scratch_shapes=[pltpu.VMEM((CHUNKS, ext, width), BF16), pltpu.SemaphoreType.DMA],
    )
    return pl.pallas_call(
        functools.partial(narrow_kernel, len(arrays), bool(sums), where),
        grid_spec=grid_spec,
        out_shape=[jax.ShapeDtypeStruct(x, F32) for x in shapes]
        + [jax.ShapeDtypeStruct((blocks, CHUNKS, ext, width), BF16)],
        input_output_aliases={len(arrays) + 3 + k: k for k in range(len(sums))},
        compiler_params=params(),
        cost_estimate=cost(
            2 * CHUNKS * rows * width * count * (columns + heads), 2 * count * width * columns
        ),
        name="project_narrow",
    )(rank, *arrays, mixing_weight, step_weight_t, *sums)


TOGETHER = 4


def owner_kernel(low, high, c_ref, s_ref, o_ref):
    p = pl.program_id(0)
    first, last = low[p], high[p]
    _, heads, head_width, state_width = s_ref.shape
    steps = c_ref.shape[1]
    channels = heads * head_width

    @pl.when(last > first)
    def _():
        state = s_ref[0].reshape(channels, state_width).astype(BF16)

        def some(g, carry):
            base = first + g * TOGETHER
            c = c_ref[pl.ds(base, TOGETHER)].astype(F32)
            c = c.reshape(TOGETHER * steps, state_width).astype(BF16)
            r = lax.dot_general(
                c, state, (((1,), (1,)), ((), ())), preferred_element_type=F32
            ).reshape(TOGETHER, steps, channels)
            for i in range(TOGETHER):

                @pl.when(base + i < last)
                def _():
                    o_ref[base + i] = r[i].astype(BF16)

            return carry

        lax.fori_loop(0, (last - first + TOGETHER - 1) // TOGETHER, some, 0)


def owner_reads(low, high, child_mix, state):
    children, steps, state_width = child_mix.shape
    children -= TOGETHER
    particles, heads, head_width, _ = state.shape
    channels = heads * head_width
    grid_spec = pltpu.PrefetchScalarGridSpec(
        num_scalar_prefetch=2,
        grid=(particles,),
        in_specs=[
            whole_spec(child_mix.shape),
            pl.BlockSpec((1, heads, head_width, state_width), lambda p, *_: (p, 0, 0, 0)),
        ],
        out_specs=whole_spec((children, steps, channels)),
    )
    return pl.pallas_call(
        owner_kernel,
        grid_spec=grid_spec,
        out_shape=jax.ShapeDtypeStruct((children, steps, channels), BF16),
        compiler_params=params(),
        cost_estimate=cost(
            2 * children * steps * channels * state_width, 4 * particles * channels * state_width
        ),
        name="owner_reads",
    )(low, high, child_mix, state)


def local_kernel(
    v_ref, rs_ref, hist_ref, tap_ref, bias_ref, b_ref, c_ref, step_ref, decay_ref, skip_ref,
    y_ref, cum_ref, dot_ref, head_width,
):
    steps, each, channels = v_ref.shape
    taps = tap_ref.shape[0]
    for t in range(steps):
        c = c_ref[t].astype(F32)
        for s in range(t + 1):
            product = jnp.sum(c * b_ref[s].astype(F32), axis=-1, keepdims=True)
            dot_ref[t * (t + 1) // 2 + s] = jnp.broadcast_to(product, (each, LANES))

    def tile(i, carry):
        at = pl.ds(pl.multiple_of(i * LANES, LANES), LANES)
        head = lax.broadcasted_iota(jnp.int32, (LANES, LANES), 0)
        lane = lax.broadcasted_iota(jnp.int32, (LANES, LANES), 1) + i * LANES
        spread = (lane // head_width == head).astype(F32)

        def expand(x):
            return jnp.dot(x, spread, precision=HIGH, preferred_element_type=F32)

        size = expand(step_ref[...]).reshape(steps, each, LANES)
        decay = expand(decay_ref[...]).reshape(steps, each, LANES)
        skip = expand(skip_ref[...])[0:1, :]
        seq = [hist_ref[k, :, at] for k in range(taps - 1)]
        seq += [v_ref[t, :, at] * rs_ref[t] for t in range(steps)]
        tap = tap_ref[:, at]
        bias = bias_ref[:, at]
        held = []
        cum = None
        for t in range(steps):
            total = bias
            for k in range(taps):
                total = total + tap[k : k + 1, :] * seq[t + k]
            value = silu(total)
            d = decay[t]
            cum = d if t == 0 else cum * d
            cum_ref[t, :, at] = cum
            held = [h * d for h in held] + [size[t] * value]
            y = skip * value
            for s in range(t + 1):
                y = y + dot_ref[t * (t + 1) // 2 + s] * held[s]
            y_ref[t, :, at] = y
        return carry

    lax.fori_loop(0, channels // LANES, tile, 0)


def local_reads(value, rs, history, taps, bias, b, c, size, decay, skip, head_width):
    steps, each, channels = value.shape
    return pl.pallas_call(
        functools.partial(local_kernel_entry, head_width),
        out_shape=[jax.ShapeDtypeStruct((steps, each, channels), F32)] * 2,
        scratch_shapes=[pltpu.VMEM((steps * (steps + 1) // 2, each, LANES), F32)],
        compiler_params=params(),
        cost_estimate=cost(steps * steps * each * channels * 16, 12 * steps * each * channels),
        name="local_reads",
    )(value, rs, history, taps, bias, b, c, size, decay, skip)


def local_kernel_entry(head_width, *refs):
    local_kernel(*refs, head_width=head_width)


def out_kernel(idx, x_ref, w_ref, o_ref):
    o_ref[0] = jnp.dot(x_ref[...], w_ref[...], preferred_element_type=F32).astype(BF16)


def project_out(idx, x, weight, width):
    rows, channels = x.shape
    count = idx.shape[0]
    grid_spec = pltpu.PrefetchScalarGridSpec(
        num_scalar_prefetch=1,
        grid=(count,),
        in_specs=[
            whole_spec((rows, channels)),
            pl.BlockSpec((channels, width), lambda i, idx: (0, idx[i])),
        ],
        out_specs=pl.BlockSpec((1, rows, width), lambda i, idx: (i, 0, 0)),
    )
    return pl.pallas_call(
        out_kernel,
        grid_spec=grid_spec,
        out_shape=jax.ShapeDtypeStruct((count, rows, width), BF16),
        compiler_params=params(),
        cost_estimate=cost(2 * rows * channels * count * width, 2 * channels * count * width),
        name="project_out",
    )(idx, x, weight)


def conv(previous, current, kernel, shift_bias):
    window = jnp.concatenate([previous, current], axis=0)
    length = current.shape[0]
    summed = jnp.zeros_like(current)
    for k in range(kernel.shape[0]):
        summed = summed + kernel[k] * window[k : k + length]
    return silu(summed + shift_bias)


def pad_lanes(x):
    return jnp.pad(x, ((0, 0), (0, LANES - x.shape[1])))


def body(
    tokens,
    parents,
    recurrent_state,
    value_history,
    mixing_history,
    input_gain,
    gate_value_weight,
    mixing_weight,
    step_weight,
    value_kernel,
    value_offset,
    mixing_kernel,
    mixing_offset,
    step_offset,
    decay_log,
    skip_gain,
    output_gain,
    output_weight,
):
    steps, particles, width = tokens.shape
    _, heads, head_width, state_width = recurrent_state.shape
    channels = heads * head_width
    each = particles // CHUNKS
    rows = steps * each
    doms = lax.axis_size("dom")
    dom = lax.axis_index("dom")
    ranks = lax.axis_size("head")
    rank = lax.axis_index("head")
    pairs = ranks // 2
    z, core = rank // 2, rank % 2
    features = width * ranks

    def permute(x, pairs_of, axis="head"):
        return lax.ppermute(x, axis, pairs_of)

    def swap(x):
        return permute(x, [(i, i ^ 1) for i in range(ranks)])

    def up(x, first, stop):
        moves = [(2 * i + c, 2 * i + 2 + c) for i in range(first, stop) for c in (0, 1)]
        return permute(x, moves)

    def down(x, first, stop):
        moves = [(2 * i + c, 2 * i - 2 + c) for i in range(first, stop) for c in (0, 1)]
        return permute(x, moves)

    def across(x, k):
        return permute(x, [(i, i ^ k) for i in range(doms)], "dom")

    prepared = prepare(tokens, input_gain)
    step_weight_t = step_weight.T

    at = rank.astype(jnp.int32).reshape(1)
    above = [prepared[k] for k in range(CHUNKS)]
    below = list(above)
    hops = [above + [swap(x) for x in above]]
    for s in range(1, pairs):
        for k in range(CHUNKS):
            above[k] = down(above[k], 1, pairs - s + 1)
            below[k] = up(below[k], s - 1, pairs - 1)
        hops.append(
            above + [swap(x) for x in above] + below + [swap(x) for x in below]
        )

    narrow = ()
    for s in range(pairs):
        where = functools.partial(place, s, pairs)
        narrow = project_narrow(
            where, ranks, at, hops[s], mixing_weight, step_weight_t, narrow
        )
    weights = ()
    for s in range(PIECES):
        weights = (split_weights(gate_value_weight, s, weights),)

    history = jnp.concatenate(
        [jnp.moveaxis(value_history, 1, 0), jnp.moveaxis(mixing_history, 1, 0)], axis=2
    ).astype(BF16)
    history, _ = lax.optimization_barrier((history, hops[1][0]))
    history_all = jnp.concatenate([history] + [across(history, k) for k in range(1, doms)], axis=1)
    first_child = dom * particles
    own_parents = lax.dynamic_slice_in_dim(parents, first_child, particles)
    held_at = ((own_parents // particles) ^ dom) * particles + own_parents % particles
    chosen = (held_at[:, None] == jnp.arange(doms * particles)[None, :]).astype(BF16)
    inherited = jnp.einsum("cp,tpw->tcw", chosen, history_all, preferred_element_type=F32)

    per_group = ranks // GROUPS
    group = rank // per_group
    columns = mixing_weight.shape[1]
    shape = (CHUNKS, steps, each)

    mix_raw, step_raw, extra, features_all = narrow
    value_all = project_wide(1, features_all, weights[0])
    gate_all = project_wide(0, features_all, weights[0])
    squares = (extra[:, 0] + extra[:, 1])[:, :rows].reshape(*shape, 1)
    rs = lax.rsqrt(squares / features + 1e-05)
    mixing = jnp.stack(
        [
            conv(
                inherited[:, k * each : (k + 1) * each, channels:],
                mix_raw[k].reshape(steps, each, columns) * rs[k],
                mixing_kernel,
                mixing_offset,
            ).astype(BF16)
            for k in range(CHUNKS)
        ]
    )
    if columns == state_width and per_group == 2:
        moves = [(g, 2 * g) for g in range(GROUPS)]
        moves += [(GROUPS + g, 2 * g + 1) for g in range(GROUPS)]
        mine = permute(mixing, moves)
        other = swap(mine)
        b_all = jnp.where(core == 0, mine, other)
        c_all = jnp.where(core == 0, other, mine)
    else:
        every = lax.all_gather(mixing, "head", axis=3, tiled=True)
        b_all = lax.dynamic_slice_in_dim(every, group * state_width, state_width, 3)
        c_all = lax.dynamic_slice_in_dim(every, (GROUPS + group) * state_width, state_width, 3)
    size_all = jax.nn.softplus(step_raw.reshape(*shape, heads) * rs + step_offset)
    decay_all = jnp.exp(-size_all * jnp.exp(decay_log))

    c_child = jnp.swapaxes(c_all, 1, 2)
    slabs = [c_child] + [across(c_child, j) for j in range(1, doms)]
    stacked = jnp.stack(slabs)
    by_dom = jnp.stack(
        [lax.dynamic_index_in_dim(stacked, dom ^ d, 0, False) for d in range(doms)]
    )

    child_mix = by_dom.reshape(doms * particles, steps, state_width)
    child_mix = jnp.pad(child_mix, ((0, TOGETHER), (0, 0), (0, 0)))
    local = parents - first_child
    held = jnp.arange(particles)[:, None]
    low = jnp.sum((local[None, :] < held).astype(jnp.int32), axis=1)
    high = jnp.sum((local[None, :] <= held).astype(jnp.int32), axis=1)
    state_reads = owner_reads(low, high, child_mix, recurrent_state)
    state_reads = state_reads.reshape(doms, CHUNKS, each, steps, channels)

    def read_states(k):
        holder = lax.dynamic_slice_in_dim(own_parents, k * each, each) // particles
        parts = [
            lax.dynamic_index_in_dim(state_reads[:, k], dom ^ j, 0, False) for j in range(doms)
        ]
        result = parts[0]
        for j in range(1, doms):
            received = across(parts[j], j)
            result = jnp.where((holder == (dom ^ j))[:, None, None], received, result)
        return jnp.moveaxis(result, 1, 0)


    def finish(k, inherited_reads):
        part = slice(k * each, (k + 1) * each)
        y, cumulative = local_reads(
            value_all[k].reshape(steps, each, channels),
            jnp.broadcast_to(rs[k], (steps, each, LANES)),
            inherited[:, part, :channels],
            value_kernel,
            value_offset.reshape(1, -1),
            b_all[k],
            c_all[k],
            pad_lanes(size_all[k].reshape(rows, heads)),
            pad_lanes(decay_all[k].reshape(rows, heads)),
            jnp.broadcast_to(pad_lanes(skip_gain.reshape(1, -1)), (8, LANES)),
            head_width,
        )
        read = cumulative * inherited_reads.astype(F32) + y
        gated = read * silu(gate_all[k].reshape(steps, each, channels) * rs[k])
        squares = jnp.sum(gated * gated, axis=2)
        total = squares
        for r in range(1, per_group):
            turn = [(i, i - i % per_group + (i + r) % per_group) for i in range(ranks)]
            total = total + permute(squares, turn)
        square_mean = total / (per_group * channels)
        return (
            (gated * lax.rsqrt(square_mean + 1e-05)[..., None] * output_gain)
            .reshape(rows, channels)
            .astype(BF16)
        )

    def scatter(scaled):
        blocks = jnp.arange(pairs, dtype=jnp.int32) * 2
        away = project_out(blocks + 1 - core, scaled, output_weight, width)
        here = project_out(blocks + core, scaled, output_weight, width)
        both = here.astype(F32) + swap(away).astype(F32)
        both = both.astype(BF16)

        def block(d):
            return lax.dynamic_index_in_dim(both, jnp.clip(d, 0, pairs - 1), 0, False).astype(F32)

        above = below = None
        for s in range(1, pairs):
            to_down = block(z - (pairs - s))
            to_up = block(z + (pairs - s))
            if s > 1:
                to_down, to_up = to_down + above.astype(F32), to_up + below.astype(F32)
            above = down(to_down.astype(BF16), pairs - s, pairs)
            below = up(to_up.astype(BF16), 0, s)
        result = block(z) + above.astype(F32) + below.astype(F32)
        return result.astype(BF16).reshape(steps, each, width)

    reads = [read_states(k) for k in range(CHUNKS)]
    outputs, scaled = [], ()
    for k in range(CHUNKS):
        inherited_reads, _ = lax.optimization_barrier((reads[k], scaled))
        scaled = finish(k, inherited_reads)
        outputs.append(scatter(scaled))
    return jnp.concatenate(outputs, axis=1)


def solution(mesh):
    return jax.shard_map(
        body,
        mesh=mesh,
        in_specs=(
            P(None, "dom", "head"),
            P(),
            P("dom", "head", None, None),
            P("dom", None, "head"),
            P("dom", None, "head"),
            P("head"),
            P(None, None, "head"),
            P(None, "head"),
            P(None, "head"),
            P(None, "head"),
            P("head"),
            P(None, "head"),
            P("head"),
            P("head"),
            P("head"),
            P("head"),
            P("head"),
            P("head", None),
        ),
        out_specs=P(None, "dom", "head"),
        check_vma=False,
    )
```

```python
import functools

import jax
import jax.numpy as jnp
from jax import lax
from jax.experimental import pallas as pl
from jax.experimental.pallas import tpu as pltpu
from jax.sharding import PartitionSpec as P


GROUPS = 4
CHUNKS = 2
LANES = 128
EXTRA = 8
PIECES = 4
HIGH = lax.Precision.HIGHEST
F32 = jnp.float32
BF16 = jnp.bfloat16


def params(mib=48):
    return pltpu.CompilerParams(vmem_limit_bytes=mib << 20)


def cost(flops, nbytes):
    return pl.CostEstimate(flops=flops, bytes_accessed=nbytes, transcendentals=0)


def whole_spec(shape):
    return pl.BlockSpec(shape, lambda *_: (0,) * len(shape))


def silu(v):
    return v / (1.0 + jnp.exp(-v))


def prepare_kernel(tok_ref, gain_ref, out_ref):
    steps, particles, width = tok_ref.shape
    count = out_ref.shape[0]
    each = particles // count
    rows = steps * each
    padded = -(-rows // LANES) * LANES
    for k in range(count):
        x = tok_ref[...].astype(F32)[:, k * each : (k + 1) * each, :].reshape(rows, width)
        out_ref[k, :rows, :] = (x * gain_ref[...]).astype(BF16)
        sq = jnp.concatenate([x * x, jnp.zeros((padded - rows, width), F32)], axis=0)
        total = lax.dot_general(
            jnp.ones((EXTRA, width), F32),
            sq,
            (((1,), (1,)), ((), ())),
            precision=HIGH,
            preferred_element_type=F32,
        )
        high = total.astype(BF16).astype(F32)
        which = lax.broadcasted_iota(jnp.int32, total.shape, 0)
        both = jnp.where(which == 0, high, jnp.where(which == 1, total - high, 0.0))
        if padded < width:
            both = jnp.concatenate([both, jnp.zeros((EXTRA, width - padded), F32)], axis=1)
        out_ref[k, rows:, :] = both.astype(BF16)


def prepare(tokens, gain):
    steps, particles, width = tokens.shape
    rows = steps * particles // CHUNKS
    return pl.pallas_call(
        prepare_kernel,
        out_shape=jax.ShapeDtypeStruct((CHUNKS, rows + EXTRA, width), BF16),
        compiler_params=params(),
        name="prepare",
    )(tokens, gain.reshape(1, -1))


def place(hop, pairs, i, rank):
    if hop == 0:
        return rank ^ i, True
    z, core = rank >> 1, rank & 1
    a, b = z + hop, z - hop
    has_a, has_b = a < pairs, b >= 0
    near = jnp.where(has_a, 2 * a + 1 - core, rank)
    far = jnp.where(has_b, 2 * b + core, near)
    from_above = jnp.where(has_a, 2 * a + (core ^ (i & 1)), far)
    from_below = jnp.where(has_b, 2 * b + (core ^ (i & 1)), near)
    return jnp.where(i < 2, from_above, from_below), jnp.where(i < 2, has_a, has_b)


def fetch_slot(valid, xs, x_ref):
    i = pl.program_id(0)
    for k in range(len(xs) // CHUNKS):

        @pl.when((i == k) & valid)
        def _():
            for chunk in range(CHUNKS):
                x_ref[chunk] = xs[CHUNKS * k + chunk][...]


def start_sums(sums, befores):
    @pl.when(pl.program_id(0) == 0)
    def _():
        for k, ref in enumerate(sums):
            ref[...] = befores[k][...] if befores else jnp.zeros_like(ref)


def narrow_kernel(count, with_sums, where, rank, *refs):
    valid = where(pl.program_id(0), rank[0])[1]
    xs, refs = refs[:count], refs[count:]
    wm_ref, ws_ref = refs[:2]
    refs = refs[2:]
    befores, refs = (refs[:4], refs[4:]) if with_sums else ((), refs)
    mix_ref, step_ref, extra_ref, all_ref, x_ref, sem = refs
    fetch_slot(valid, xs, x_ref)
    start_sums((mix_ref, step_ref, extra_ref), befores)
    rows = mix_ref.shape[1]

    @pl.when(valid)
    def _():
        for k in range(CHUNKS):
            x = x_ref[k, :rows, :]
            mix_ref[k] += jnp.dot(x, wm_ref[...], preferred_element_type=F32)
            step_ref[k] += lax.dot_general(
                x, ws_ref[...], (((1,), (1,)), ((), ())), preferred_element_type=F32
            )
            extra_ref[k] += x_ref[k, rows:, :].astype(F32)
        block = where(pl.program_id(0), rank[0])[0]
        copy = pltpu.make_async_copy(x_ref, all_ref.at[block], sem)
        copy.start()
        copy.wait()


def split_kernel(*refs):
    w_ref, o_ref = refs[0], refs[-1]
    depth, _, width = w_ref.shape
    half = min(LANES, depth)
    row = lax.broadcasted_iota(jnp.int32, (2 * half, 2 * half), 0)
    col = lax.broadcasted_iota(jnp.int32, (2 * half, 2 * half), 1)
    source = jnp.where(row < half, 2 * row, 2 * (row - half) + 1)
    move = (source == col).astype(F32).astype(BF16)
    for i in range(depth // half):
        part = w_ref[i * half : (i + 1) * half].reshape(2 * half, width)
        moved = jnp.dot(move, part, preferred_element_type=F32).astype(BF16)
        o_ref[0, i * half : (i + 1) * half, :] = moved[:half]
        o_ref[1, i * half : (i + 1) * half, :] = moved[half:]


def split_weights(w, piece, before):
    depth, _, width = w.shape
    block = depth // (2 * PIECES)
    return pl.pallas_call(
        split_kernel,
        grid=(2,),
        in_specs=[pl.BlockSpec((block, 2, width), lambda k: (2 * piece + k, 0, 0))]
        + [pl.BlockSpec(memory_space=pl.ANY)] * len(before),
        out_specs=pl.BlockSpec((2, block, width), lambda k: (0, 2 * piece + k, 0)),
        out_shape=jax.ShapeDtypeStruct((2, depth, width), BF16),
        input_output_aliases={1 + k: k for k in range(len(before))},
        compiler_params=params(),
        cost_estimate=cost(4 * block * width * 512, 16 * block * width),
        name="split_weights",
    )(w, *before)


def wide_kernel(x_ref, w_ref, o_ref):
    rows = o_ref.shape[1]
    depth = w_ref.shape[1]
    x = x_ref[0, :, :rows, :].astype(F32).reshape(CHUNKS * rows, depth).astype(BF16)
    y = jnp.dot(x, w_ref[0], preferred_element_type=F32).reshape(o_ref.shape)

    @pl.when(pl.program_id(0) == 0)
    def _():
        o_ref[...] = y

    @pl.when(pl.program_id(0) > 0)
    def _():
        o_ref[...] += y


def project_wide(which, features, weights):
    blocks, _, ext, width = features.shape
    rows = ext - EXTRA
    channels = weights.shape[2]
    shape = (CHUNKS, rows, channels)
    return pl.pallas_call(
        wide_kernel,
        grid=(blocks,),
        in_specs=[
            pl.BlockSpec((1, CHUNKS, ext, width), lambda i: (i, 0, 0, 0)),
            pl.BlockSpec((1, width, channels), lambda i: (which, i, 0)),
        ],
        out_specs=whole_spec(shape),
        out_shape=jax.ShapeDtypeStruct(shape, F32),
        compiler_params=params(),
        cost_estimate=cost(
            2 * CHUNKS * rows * width * blocks * channels, 2 * blocks * width * channels
        ),
        name="project_wide",
    )(features, weights)


def project_narrow(where, blocks, rank, arrays, mixing_weight, step_weight_t, sums):
    ext, width = arrays[0].shape
    rows = ext - EXTRA
    columns, heads = mixing_weight.shape[1], step_weight_t.shape[0]
    count = len(arrays) // CHUNKS
    shapes = [(CHUNKS, rows, columns), (CHUNKS, rows, heads), (CHUNKS, EXTRA, width)]
    anywhere = pl.BlockSpec(memory_space=pl.ANY)
    grid_spec = pltpu.PrefetchScalarGridSpec(
        num_scalar_prefetch=1,
        grid=(count,),
        in_specs=[whole_spec((ext, width))] * len(arrays)
        + [
            pl.BlockSpec((width, columns), lambda i, rank: (where(i, rank[0])[0], 0)),
            pl.BlockSpec((heads, width), lambda i, rank: (0, where(i, rank[0])[0])),
        ]
        + [whole_spec(x.shape) for x in sums[:3]]
        + [anywhere] * len(sums[3:]),
        out_specs=[whole_spec(x) for x in shapes] + [anywhere],
        scratch_shapes=[pltpu.VMEM((CHUNKS, ext, width), BF16), pltpu.SemaphoreType.DMA],
    )
    return pl.pallas_call(
        functools.partial(narrow_kernel, len(arrays), bool(sums), where),
        grid_spec=grid_spec,
        out_shape=[jax.ShapeDtypeStruct(x, F32) for x in shapes]
        + [jax.ShapeDtypeStruct((blocks, CHUNKS, ext, width), BF16)],
        input_output_aliases={len(arrays) + 3 + k: k for k in range(len(sums))},
        compiler_params=params(),
        cost_estimate=cost(
            2 * CHUNKS * rows * width * count * (columns + heads), 2 * count * width * columns
        ),
        name="project_narrow",
    )(rank, *arrays, mixing_weight, step_weight_t, *sums)


TOGETHER = 4
HELD = 4


def owner_kernel(low, high, c_ref, s_ref, o_ref):
    held, heads, head_width, state_width = s_ref.shape
    steps = c_ref.shape[1]
    channels = heads * head_width

    def one(q, carry):
        p = pl.program_id(0) * held + q
        first, last = low[p], high[p]

        @pl.when(last > first)
        def _():
            state = s_ref[q].reshape(channels, state_width).astype(BF16)

            def some(g, carry):
                base = first + g * TOGETHER
                c = c_ref[pl.ds(base, TOGETHER)].astype(F32)
                c = c.reshape(TOGETHER * steps, state_width).astype(BF16)
                r = lax.dot_general(
                    c, state, (((1,), (1,)), ((), ())), preferred_element_type=F32
                ).reshape(TOGETHER, steps, channels)
                for i in range(TOGETHER):

                    @pl.when(base + i < last)
                    def _():
                        o_ref[base + i] = r[i].astype(BF16)

                return carry

            lax.fori_loop(0, (last - first + TOGETHER - 1) // TOGETHER, some, 0)

        return carry

    lax.fori_loop(0, held, one, 0)


def owner_reads(low, high, child_mix, state):
    children, steps, state_width = child_mix.shape
    children -= TOGETHER
    particles, heads, head_width, _ = state.shape
    channels = heads * head_width
    grid_spec = pltpu.PrefetchScalarGridSpec(
        num_scalar_prefetch=2,
        grid=(particles // HELD,),
        in_specs=[
            whole_spec(child_mix.shape),
            pl.BlockSpec((HELD, heads, head_width, state_width), lambda p, *_: (p, 0, 0, 0)),
        ],
        out_specs=whole_spec((children, steps, channels)),
    )
    return pl.pallas_call(
        owner_kernel,
        grid_spec=grid_spec,
        out_shape=jax.ShapeDtypeStruct((children, steps, channels), BF16),
        compiler_params=params(),
        cost_estimate=cost(
            2 * children * steps * channels * state_width, 4 * particles * channels * state_width
        ),
        name="owner_reads",
    )(low, high, child_mix, state)


def local_kernel(
    v_ref, rs_ref, hist_ref, tap_ref, bias_ref, b_ref, c_ref, step_ref, decay_ref, skip_ref,
    y_ref, cum_ref, dot_ref, head_width,
):
    steps, each, channels = v_ref.shape
    taps = tap_ref.shape[0]
    for t in range(steps):
        c = c_ref[t].astype(F32)
        for s in range(t + 1):
            product = jnp.sum(c * b_ref[s].astype(F32), axis=-1, keepdims=True)
            dot_ref[t * (t + 1) // 2 + s] = jnp.broadcast_to(product, (each, LANES))

    def tile(i, carry):
        at = pl.ds(pl.multiple_of(i * LANES, LANES), LANES)
        head = lax.broadcasted_iota(jnp.int32, (LANES, LANES), 0)
        lane = lax.broadcasted_iota(jnp.int32, (LANES, LANES), 1) + i * LANES
        spread = (lane // head_width == head).astype(F32)

        def expand(x):
            return jnp.dot(x, spread, precision=HIGH, preferred_element_type=F32)

        size = expand(step_ref[...]).reshape(steps, each, LANES)
        decay = expand(decay_ref[...]).reshape(steps, each, LANES)
        skip = expand(skip_ref[...])[0:1, :]
        seq = [hist_ref[k, :, at] for k in range(taps - 1)]
        seq += [v_ref[t, :, at] * rs_ref[t] for t in range(steps)]
        tap = tap_ref[:, at]
        bias = bias_ref[:, at]
        held = []
        cum = None
        for t in range(steps):
            total = bias
            for k in range(taps):
                total = total + tap[k : k + 1, :] * seq[t + k]
            value = silu(total)
            d = decay[t]
            cum = d if t == 0 else cum * d
            cum_ref[t, :, at] = cum
            held = [h * d for h in held] + [size[t] * value]
            y = skip * value
            for s in range(t + 1):
                y = y + dot_ref[t * (t + 1) // 2 + s] * held[s]
            y_ref[t, :, at] = y
        return carry

    lax.fori_loop(0, channels // LANES, tile, 0)


def local_reads(value, rs, history, taps, bias, b, c, size, decay, skip, head_width):
    steps, each, channels = value.shape
    return pl.pallas_call(
        functools.partial(local_kernel_entry, head_width),
        out_shape=[jax.ShapeDtypeStruct((steps, each, channels), F32)] * 2,
        scratch_shapes=[pltpu.VMEM((steps * (steps + 1) // 2, each, LANES), F32)],
        compiler_params=params(),
        cost_estimate=cost(steps * steps * each * channels * 16, 12 * steps * each * channels),
        name="local_reads",
    )(value, rs, history, taps, bias, b, c, size, decay, skip)


def local_kernel_entry(head_width, *refs):
    local_kernel(*refs, head_width=head_width)


def out_kernel(idx, x_ref, w_ref, o_ref):
    o_ref[0] = jnp.dot(x_ref[...], w_ref[...], preferred_element_type=F32).astype(BF16)


def project_out(idx, x, weight, width):
    rows, channels = x.shape
    count = idx.shape[0]
    grid_spec = pltpu.PrefetchScalarGridSpec(
        num_scalar_prefetch=1,
        grid=(count,),
        in_specs=[
            whole_spec((rows, channels)),
            pl.BlockSpec((channels, width), lambda i, idx: (0, idx[i])),
        ],
        out_specs=pl.BlockSpec((1, rows, width), lambda i, idx: (i, 0, 0)),
    )
    return pl.pallas_call(
        out_kernel,
        grid_spec=grid_spec,
        out_shape=jax.ShapeDtypeStruct((count, rows, width), BF16),
        compiler_params=params(),
        cost_estimate=cost(2 * rows * channels * count * width, 2 * channels * count * width),
        name="project_out",
    )(idx, x, weight)


def conv(previous, current, kernel, shift_bias):
    window = jnp.concatenate([previous, current], axis=0)
    length = current.shape[0]
    summed = jnp.zeros_like(current)
    for k in range(kernel.shape[0]):
        summed = summed + kernel[k] * window[k : k + length]
    return silu(summed + shift_bias)


def pad_lanes(x):
    return jnp.pad(x, ((0, 0), (0, LANES - x.shape[1])))


def body(
    tokens,
    parents,
    recurrent_state,
    value_history,
    mixing_history,
    input_gain,
    gate_value_weight,
    mixing_weight,
    step_weight,
    value_kernel,
    value_offset,
    mixing_kernel,
    mixing_offset,
    step_offset,
    decay_log,
    skip_gain,
    output_gain,
    output_weight,
):
    steps, particles, width = tokens.shape
    _, heads, head_width, state_width = recurrent_state.shape
    channels = heads * head_width
    each = particles // CHUNKS
    rows = steps * each
    doms = lax.axis_size("dom")
    dom = lax.axis_index("dom")
    ranks = lax.axis_size("head")
    rank = lax.axis_index("head")
    pairs = ranks // 2
    z, core = rank // 2, rank % 2
    features = width * ranks

    def permute(x, pairs_of, axis="head"):
        return lax.ppermute(x, axis, pairs_of)

    def swap(x):
        return permute(x, [(i, i ^ 1) for i in range(ranks)])

    def up(x, first, stop):
        moves = [(2 * i + c, 2 * i + 2 + c) for i in range(first, stop) for c in (0, 1)]
        return permute(x, moves)

    def down(x, first, stop):
        moves = [(2 * i + c, 2 * i - 2 + c) for i in range(first, stop) for c in (0, 1)]
        return permute(x, moves)

    def across(x, k):
        return permute(x, [(i, i ^ k) for i in range(doms)], "dom")

    prepared = prepare(tokens, input_gain)
    step_weight_t = step_weight.T

    at = rank.astype(jnp.int32).reshape(1)
    above = [prepared[k] for k in range(CHUNKS)]
    below = list(above)
    hops = [above + [swap(x) for x in above]]
    for s in range(1, pairs):
        for k in range(CHUNKS):
            above[k] = down(above[k], 1, pairs - s + 1)
            below[k] = up(below[k], s - 1, pairs - 1)
        hops.append(
            above + [swap(x) for x in above] + below + [swap(x) for x in below]
        )

    narrow = ()
    for s in range(pairs):
        where = functools.partial(place, s, pairs)
        narrow = project_narrow(
            where, ranks, at, hops[s], mixing_weight, step_weight_t, narrow
        )
    weights = ()
    for s in range(PIECES):
        weights = (split_weights(gate_value_weight, s, weights),)

    history = jnp.concatenate(
        [jnp.moveaxis(value_history, 1, 0), jnp.moveaxis(mixing_history, 1, 0)], axis=2
    ).astype(BF16)
    history, _ = lax.optimization_barrier((history, hops[1][0]))
    history_all = jnp.concatenate([history] + [across(history, k) for k in range(1, doms)], axis=1)
    first_child = dom * particles
    own_parents = lax.dynamic_slice_in_dim(parents, first_child, particles)
    held_at = ((own_parents // particles) ^ dom) * particles + own_parents % particles
    chosen = (held_at[:, None] == jnp.arange(doms * particles)[None, :]).astype(BF16)
    inherited = jnp.einsum("cp,tpw->tcw", chosen, history_all, preferred_element_type=F32)

    per_group = ranks // GROUPS
    group = rank // per_group
    columns = mixing_weight.shape[1]
    shape = (CHUNKS, steps, each)

    mix_raw, step_raw, extra, features_all = narrow
    value_all = project_wide(1, features_all, weights[0])
    gate_all = project_wide(0, features_all, weights[0])
    squares = (extra[:, 0] + extra[:, 1])[:, :rows].reshape(*shape, 1)
    rs = lax.rsqrt(squares / features + 1e-05)
    mixing = jnp.stack(
        [
            conv(
                inherited[:, k * each : (k + 1) * each, channels:],
                mix_raw[k].reshape(steps, each, columns) * rs[k],
                mixing_kernel,
                mixing_offset,
            ).astype(BF16)
            for k in range(CHUNKS)
        ]
    )
    if columns == state_width and per_group == 2:
        moves = [(g, 2 * g) for g in range(GROUPS)]
        moves += [(GROUPS + g, 2 * g + 1) for g in range(GROUPS)]
        mine = permute(mixing, moves)
        other = swap(mine)
        b_all = jnp.where(core == 0, mine, other)
        c_all = jnp.where(core == 0, other, mine)
    else:
        every = lax.all_gather(mixing, "head", axis=3, tiled=True)
        b_all = lax.dynamic_slice_in_dim(every, group * state_width, state_width, 3)
        c_all = lax.dynamic_slice_in_dim(every, (GROUPS + group) * state_width, state_width, 3)
    size_all = jax.nn.softplus(step_raw.reshape(*shape, heads) * rs + step_offset)
    decay_all = jnp.exp(-size_all * jnp.exp(decay_log))

    c_child = jnp.swapaxes(c_all, 1, 2)
    slabs = [c_child] + [across(c_child, j) for j in range(1, doms)]
    stacked = jnp.stack(slabs)
    by_dom = jnp.stack(
        [lax.dynamic_index_in_dim(stacked, dom ^ d, 0, False) for d in range(doms)]
    )

    child_mix = by_dom.reshape(doms * particles, steps, state_width)
    child_mix = jnp.pad(child_mix, ((0, TOGETHER), (0, 0), (0, 0)))
    local = parents - first_child
    held = jnp.arange(particles)[:, None]
    low = jnp.sum((local[None, :] < held).astype(jnp.int32), axis=1)
    high = jnp.sum((local[None, :] <= held).astype(jnp.int32), axis=1)
    state_reads = owner_reads(low, high, child_mix, recurrent_state)
    state_reads = state_reads.reshape(doms, CHUNKS, each, steps, channels)

    def read_states(k):
        holder = lax.dynamic_slice_in_dim(own_parents, k * each, each) // particles
        parts = [
            lax.dynamic_index_in_dim(state_reads[:, k], dom ^ j, 0, False) for j in range(doms)
        ]
        result = parts[0]
        for j in range(1, doms):
            received = across(parts[j], j)
            result = jnp.where((holder == (dom ^ j))[:, None, None], received, result)
        return jnp.moveaxis(result, 1, 0)


    def finish(k, inherited_reads):
        part = slice(k * each, (k + 1) * each)
        y, cumulative = local_reads(
            value_all[k].reshape(steps, each, channels),
            jnp.broadcast_to(rs[k], (steps, each, LANES)),
            inherited[:, part, :channels],
            value_kernel,
            value_offset.reshape(1, -1),
            b_all[k],
            c_all[k],
            pad_lanes(size_all[k].reshape(rows, heads)),
            pad_lanes(decay_all[k].reshape(rows, heads)),
            jnp.broadcast_to(pad_lanes(skip_gain.reshape(1, -1)), (8, LANES)),
            head_width,
        )
        read = cumulative * inherited_reads.astype(F32) + y
        gated = read * silu(gate_all[k].reshape(steps, each, channels) * rs[k])
        squares = jnp.sum(gated * gated, axis=2)
        total = squares
        for r in range(1, per_group):
            turn = [(i, i - i % per_group + (i + r) % per_group) for i in range(ranks)]
            total = total + permute(squares, turn)
        square_mean = total / (per_group * channels)
        return (
            (gated * lax.rsqrt(square_mean + 1e-05)[..., None] * output_gain)
            .reshape(rows, channels)
            .astype(BF16)
        )

    def scatter(scaled):
        blocks = jnp.arange(pairs, dtype=jnp.int32) * 2
        away = project_out(blocks + 1 - core, scaled, output_weight, width)
        here = project_out(blocks + core, scaled, output_weight, width)
        both = here.astype(F32) + swap(away).astype(F32)
        both = both.astype(BF16)

        def block(d):
            return lax.dynamic_index_in_dim(both, jnp.clip(d, 0, pairs - 1), 0, False).astype(F32)

        above = below = None
        for s in range(1, pairs):
            to_down = block(z - (pairs - s))
            to_up = block(z + (pairs - s))
            if s > 1:
                to_down, to_up = to_down + above.astype(F32), to_up + below.astype(F32)
            above = down(to_down.astype(BF16), pairs - s, pairs)
            below = up(to_up.astype(BF16), 0, s)
        result = block(z) + above.astype(F32) + below.astype(F32)
        return result.astype(BF16).reshape(steps, each, width)

    reads = [read_states(k) for k in range(CHUNKS)]
    outputs, scaled = [], ()
    for k in range(CHUNKS):
        inherited_reads, _ = lax.optimization_barrier((reads[k], scaled))
        scaled = finish(k, inherited_reads)
        outputs.append(scatter(scaled))
    return jnp.concatenate(outputs, axis=1)


def solution(mesh):
    return jax.shard_map(
        body,
        mesh=mesh,
        in_specs=(
            P(None, "dom", "head"),
            P(),
            P("dom", "head", None, None),
            P("dom", None, "head"),
            P("dom", None, "head"),
            P("head"),
            P(None, None, "head"),
            P(None, "head"),
            P(None, "head"),
            P(None, "head"),
            P("head"),
            P(None, "head"),
            P("head"),
            P("head"),
            P("head"),
            P("head"),
            P("head"),
            P("head", None),
        ),
        out_specs=P(None, "dom", "head"),
        check_vma=False,
    )
```

```python
import functools

import jax
import jax.numpy as jnp
from jax import lax
from jax.experimental import pallas as pl
from jax.experimental.pallas import tpu as pltpu
from jax.sharding import PartitionSpec as P


GROUPS = 4
CHUNKS = 2
LANES = 128
EXTRA = 8
PIECES = 4
HIGH = lax.Precision.HIGHEST
F32 = jnp.float32
BF16 = jnp.bfloat16


def params(mib=48):
    return pltpu.CompilerParams(vmem_limit_bytes=mib << 20)


def cost(flops, nbytes):
    return pl.CostEstimate(flops=flops, bytes_accessed=nbytes, transcendentals=0)


def whole_spec(shape):
    return pl.BlockSpec(shape, lambda *_: (0,) * len(shape))


def silu(v):
    return v / (1.0 + jnp.exp(-v))


def prepare_kernel(tok_ref, gain_ref, out_ref):
    steps, particles, width = tok_ref.shape
    count = out_ref.shape[0]
    each = particles // count
    rows = steps * each
    padded = -(-rows // LANES) * LANES
    for k in range(count):
        x = tok_ref[...].astype(F32)[:, k * each : (k + 1) * each, :].reshape(rows, width)
        out_ref[k, :rows, :] = (x * gain_ref[...]).astype(BF16)
        sq = jnp.concatenate([x * x, jnp.zeros((padded - rows, width), F32)], axis=0)
        total = lax.dot_general(
            jnp.ones((EXTRA, width), F32),
            sq,
            (((1,), (1,)), ((), ())),
            precision=HIGH,
            preferred_element_type=F32,
        )
        high = total.astype(BF16).astype(F32)
        which = lax.broadcasted_iota(jnp.int32, total.shape, 0)
        both = jnp.where(which == 0, high, jnp.where(which == 1, total - high, 0.0))
        if padded < width:
            both = jnp.concatenate([both, jnp.zeros((EXTRA, width - padded), F32)], axis=1)
        out_ref[k, rows:, :] = both.astype(BF16)


def prepare(tokens, gain):
    steps, particles, width = tokens.shape
    rows = steps * particles // CHUNKS
    return pl.pallas_call(
        prepare_kernel,
        out_shape=jax.ShapeDtypeStruct((CHUNKS, rows + EXTRA, width), BF16),
        compiler_params=params(),
        name="prepare",
    )(tokens, gain.reshape(1, -1))


def place(hop, pairs, i, rank):
    if hop == 0:
        return rank ^ i, True
    z, core = rank >> 1, rank & 1
    a, b = z + hop, z - hop
    has_a, has_b = a < pairs, b >= 0
    near = jnp.where(has_a, 2 * a + 1 - core, rank)
    far = jnp.where(has_b, 2 * b + core, near)
    from_above = jnp.where(has_a, 2 * a + (core ^ (i & 1)), far)
    from_below = jnp.where(has_b, 2 * b + (core ^ (i & 1)), near)
    return jnp.where(i < 2, from_above, from_below), jnp.where(i < 2, has_a, has_b)


def fetch_slot(valid, xs, x_ref):
    i = pl.program_id(0)
    for k in range(len(xs) // CHUNKS):

        @pl.when((i == k) & valid)
        def _():
            for chunk in range(CHUNKS):
                x_ref[chunk] = xs[CHUNKS * k + chunk][...]


def start_sums(sums, befores):
    @pl.when(pl.program_id(0) == 0)
    def _():
        for k, ref in enumerate(sums):
            ref[...] = befores[k][...] if befores else jnp.zeros_like(ref)


def narrow_kernel(count, with_sums, where, rank, *refs):
    valid = where(pl.program_id(0), rank[0])[1]
    xs, refs = refs[:count], refs[count:]
    wm_ref, ws_ref = refs[:2]
    refs = refs[2:]
    befores, refs = (refs[:4], refs[4:]) if with_sums else ((), refs)
    mix_ref, step_ref, extra_ref, all_ref, x_ref, sem = refs
    fetch_slot(valid, xs, x_ref)
    start_sums((mix_ref, step_ref, extra_ref), befores)
    rows = mix_ref.shape[1]

    @pl.when(valid)
    def _():
        for k in range(CHUNKS):
            x = x_ref[k, :rows, :]
            mix_ref[k] += jnp.dot(x, wm_ref[...], preferred_element_type=F32)
            step_ref[k] += lax.dot_general(
                x, ws_ref[...], (((1,), (1,)), ((), ())), preferred_element_type=F32
            )
            extra_ref[k] += x_ref[k, rows:, :].astype(F32)
        block = where(pl.program_id(0), rank[0])[0]
        copy = pltpu.make_async_copy(x_ref, all_ref.at[block], sem)
        copy.start()
        copy.wait()


def split_kernel(*refs):
    w_ref, o_ref = refs[0], refs[-1]
    depth, _, width = w_ref.shape
    half = min(LANES, depth)
    row = lax.broadcasted_iota(jnp.int32, (2 * half, 2 * half), 0)
    col = lax.broadcasted_iota(jnp.int32, (2 * half, 2 * half), 1)
    source = jnp.where(row < half, 2 * row, 2 * (row - half) + 1)
    move = (source == col).astype(F32).astype(BF16)
    for i in range(depth // half):
        part = w_ref[i * half : (i + 1) * half].reshape(2 * half, width)
        moved = jnp.dot(move, part, preferred_element_type=F32).astype(BF16)
        o_ref[0, i * half : (i + 1) * half, :] = moved[:half]
        o_ref[1, i * half : (i + 1) * half, :] = moved[half:]


def split_weights(w, piece, before):
    depth, _, width = w.shape
    block = depth // (2 * PIECES)
    return pl.pallas_call(
        split_kernel,
        grid=(2,),
        in_specs=[pl.BlockSpec((block, 2, width), lambda k: (2 * piece + k, 0, 0))]
        + [pl.BlockSpec(memory_space=pl.ANY)] * len(before),
        out_specs=pl.BlockSpec((2, block, width), lambda k: (0, 2 * piece + k, 0)),
        out_shape=jax.ShapeDtypeStruct((2, depth, width), BF16),
        input_output_aliases={1 + k: k for k in range(len(before))},
        compiler_params=params(),
        cost_estimate=cost(4 * block * width * 512, 16 * block * width),
        name="split_weights",
    )(w, *before)


def wide_kernel(x_ref, w_ref, o_ref):
    rows = o_ref.shape[1]
    depth = w_ref.shape[1]
    x = x_ref[0, :, :rows, :].astype(F32).reshape(CHUNKS * rows, depth).astype(BF16)
    y = jnp.dot(x, w_ref[0], preferred_element_type=F32).reshape(o_ref.shape)

    @pl.when(pl.program_id(0) == 0)
    def _():
        o_ref[...] = y

    @pl.when(pl.program_id(0) > 0)
    def _():
        o_ref[...] += y


def project_wide(which, features, weights):
    blocks, _, ext, width = features.shape
    rows = ext - EXTRA
    channels = weights.shape[2]
    shape = (CHUNKS, rows, channels)
    return pl.pallas_call(
        wide_kernel,
        grid=(blocks,),
        in_specs=[
            pl.BlockSpec((1, CHUNKS, ext, width), lambda i: (i, 0, 0, 0)),
            pl.BlockSpec((1, width, channels), lambda i: (which, i, 0)),
        ],
        out_specs=whole_spec(shape),
        out_shape=jax.ShapeDtypeStruct(shape, F32),
        compiler_params=params(),
        cost_estimate=cost(
            2 * CHUNKS * rows * width * blocks * channels, 2 * blocks * width * channels
        ),
        name="project_wide",
    )(features, weights)


def project_narrow(where, blocks, rank, arrays, mixing_weight, step_weight_t, sums):
    ext, width = arrays[0].shape
    rows = ext - EXTRA
    columns, heads = mixing_weight.shape[1], step_weight_t.shape[0]
    count = len(arrays) // CHUNKS
    shapes = [(CHUNKS, rows, columns), (CHUNKS, rows, heads), (CHUNKS, EXTRA, width)]
    anywhere = pl.BlockSpec(memory_space=pl.ANY)
    grid_spec = pltpu.PrefetchScalarGridSpec(
        num_scalar_prefetch=1,
        grid=(count,),
        in_specs=[whole_spec((ext, width))] * len(arrays)
        + [
            pl.BlockSpec((width, columns), lambda i, rank: (where(i, rank[0])[0], 0)),
            pl.BlockSpec((heads, width), lambda i, rank: (0, where(i, rank[0])[0])),
        ]
        + [whole_spec(x.shape) for x in sums[:3]]
        + [anywhere] * len(sums[3:]),
        out_specs=[whole_spec(x) for x in shapes] + [anywhere],
        scratch_shapes=[pltpu.VMEM((CHUNKS, ext, width), BF16), pltpu.SemaphoreType.DMA],
    )
    return pl.pallas_call(
        functools.partial(narrow_kernel, len(arrays), bool(sums), where),
        grid_spec=grid_spec,
        out_shape=[jax.ShapeDtypeStruct(x, F32) for x in shapes]
        + [jax.ShapeDtypeStruct((blocks, CHUNKS, ext, width), BF16)],
        input_output_aliases={len(arrays) + 3 + k: k for k in range(len(sums))},
        compiler_params=params(),
        cost_estimate=cost(
            2 * CHUNKS * rows * width * count * (columns + heads), 2 * count * width * columns
        ),
        name="project_narrow",
    )(rank, *arrays, mixing_weight, step_weight_t, *sums)


TOGETHER = 4
HELD = 4


def owner_kernel(low, high, c_ref, s_ref, o_ref):
    held, heads, head_width, state_width = s_ref.shape
    steps = c_ref.shape[1]
    channels = heads * head_width

    def one(q, carry):
        p = pl.program_id(0) * held + q
        first, last = low[p], high[p]

        @pl.when(last > first)
        def _():
            state = s_ref[q].reshape(channels, state_width).astype(BF16)

            def some(g, carry):
                base = first + g * TOGETHER
                c = c_ref[pl.ds(base, TOGETHER)].astype(F32)
                c = c.reshape(TOGETHER * steps, state_width).astype(BF16)
                r = lax.dot_general(
                    c, state, (((1,), (1,)), ((), ())), preferred_element_type=F32
                ).reshape(TOGETHER, steps, channels)
                for i in range(TOGETHER):

                    @pl.when(base + i < last)
                    def _():
                        o_ref[base + i] = r[i].astype(BF16)

                return carry

            lax.fori_loop(0, (last - first + TOGETHER - 1) // TOGETHER, some, 0)

        return carry

    lax.fori_loop(0, held, one, 0)


def owner_reads(low, high, child_mix, state):
    children, steps, state_width = child_mix.shape
    children -= TOGETHER
    particles, heads, head_width, _ = state.shape
    channels = heads * head_width
    grid_spec = pltpu.PrefetchScalarGridSpec(
        num_scalar_prefetch=2,
        grid=(particles // HELD,),
        in_specs=[
            whole_spec(child_mix.shape),
            pl.BlockSpec((HELD, heads, head_width, state_width), lambda p, *_: (p, 0, 0, 0)),
        ],
        out_specs=whole_spec((children, steps, channels)),
    )
    return pl.pallas_call(
        owner_kernel,
        grid_spec=grid_spec,
        out_shape=jax.ShapeDtypeStruct((children, steps, channels), BF16),
        compiler_params=params(),
        cost_estimate=cost(
            2 * children * steps * channels * state_width, 4 * particles * channels * state_width
        ),
        name="owner_reads",
    )(low, high, child_mix, state)


def local_kernel(
    v_ref, rs_ref, hist_ref, tap_ref, bias_ref, b_ref, c_ref, step_ref, decay_ref, skip_ref,
    y_ref, cum_ref, dot_ref, head_width,
):
    steps, each, channels = v_ref.shape
    taps = tap_ref.shape[0]
    for t in range(steps):
        c = c_ref[t].astype(F32)
        for s in range(t + 1):
            product = jnp.sum(c * b_ref[s].astype(F32), axis=-1, keepdims=True)
            dot_ref[t * (t + 1) // 2 + s] = jnp.broadcast_to(product, (each, LANES))

    def tile(i, carry):
        at = pl.ds(pl.multiple_of(i * LANES, LANES), LANES)
        head = lax.broadcasted_iota(jnp.int32, (LANES, LANES), 0)
        lane = lax.broadcasted_iota(jnp.int32, (LANES, LANES), 1) + i * LANES
        spread = (lane // head_width == head).astype(F32)

        def expand(x):
            return jnp.dot(x, spread, precision=HIGH, preferred_element_type=F32)

        size = expand(step_ref[...]).reshape(steps, each, LANES)
        decay = expand(decay_ref[...]).reshape(steps, each, LANES)
        skip = expand(skip_ref[...])[0:1, :]
        seq = [hist_ref[k, :, at] for k in range(taps - 1)]
        seq += [v_ref[t, :, at] * rs_ref[t] for t in range(steps)]
        tap = tap_ref[:, at]
        bias = bias_ref[:, at]
        held = []
        cum = None
        for t in range(steps):
            total = bias
            for k in range(taps):
                total = total + tap[k : k + 1, :] * seq[t + k]
            value = silu(total)
            d = decay[t]
            cum = d if t == 0 else cum * d
            cum_ref[t, :, at] = cum
            held = [h * d for h in held] + [size[t] * value]
            y = skip * value
            for s in range(t + 1):
                y = y + dot_ref[t * (t + 1) // 2 + s] * held[s]
            y_ref[t, :, at] = y
        return carry

    lax.fori_loop(0, channels // LANES, tile, 0)


def local_reads(value, rs, history, taps, bias, b, c, size, decay, skip, head_width):
    steps, each, channels = value.shape
    return pl.pallas_call(
        functools.partial(local_kernel_entry, head_width),
        out_shape=[jax.ShapeDtypeStruct((steps, each, channels), F32)] * 2,
        scratch_shapes=[pltpu.VMEM((steps * (steps + 1) // 2, each, LANES), F32)],
        compiler_params=params(),
        cost_estimate=cost(steps * steps * each * channels * 16, 12 * steps * each * channels),
        name="local_reads",
    )(value, rs, history, taps, bias, b, c, size, decay, skip)


def local_kernel_entry(head_width, *refs):
    local_kernel(*refs, head_width=head_width)


def out_kernel(idx, x_ref, w_ref, o_ref):
    o_ref[0] = jnp.dot(x_ref[...], w_ref[...], preferred_element_type=F32).astype(BF16)


def project_out(idx, x, weight, width):
    rows, channels = x.shape
    count = idx.shape[0]
    grid_spec = pltpu.PrefetchScalarGridSpec(
        num_scalar_prefetch=1,
        grid=(count,),
        in_specs=[
            whole_spec((rows, channels)),
            pl.BlockSpec((channels, width), lambda i, idx: (0, idx[i])),
        ],
        out_specs=pl.BlockSpec((1, rows, width), lambda i, idx: (i, 0, 0)),
    )
    return pl.pallas_call(
        out_kernel,
        grid_spec=grid_spec,
        out_shape=jax.ShapeDtypeStruct((count, rows, width), BF16),
        compiler_params=params(),
        cost_estimate=cost(2 * rows * channels * count * width, 2 * channels * count * width),
        name="project_out",
    )(idx, x, weight)


def conv(previous, current, kernel, shift_bias):
    window = jnp.concatenate([previous, current], axis=0)
    length = current.shape[0]
    summed = jnp.zeros_like(current)
    for k in range(kernel.shape[0]):
        summed = summed + kernel[k] * window[k : k + length]
    return silu(summed + shift_bias)


def pad_lanes(x):
    return jnp.pad(x, ((0, 0), (0, LANES - x.shape[1])))


def body(
    tokens,
    parents,
    recurrent_state,
    value_history,
    mixing_history,
    input_gain,
    gate_value_weight,
    mixing_weight,
    step_weight,
    value_kernel,
    value_offset,
    mixing_kernel,
    mixing_offset,
    step_offset,
    decay_log,
    skip_gain,
    output_gain,
    output_weight,
):
    steps, particles, width = tokens.shape
    _, heads, head_width, state_width = recurrent_state.shape
    channels = heads * head_width
    each = particles // CHUNKS
    rows = steps * each
    doms = lax.axis_size("dom")
    dom = lax.axis_index("dom")
    ranks = lax.axis_size("head")
    rank = lax.axis_index("head")
    pairs = ranks // 2
    z, core = rank // 2, rank % 2
    features = width * ranks

    def permute(x, pairs_of, axis="head"):
        return lax.ppermute(x, axis, pairs_of)

    def swap(x):
        return permute(x, [(i, i ^ 1) for i in range(ranks)])

    def up(x, first, stop):
        moves = [(2 * i + c, 2 * i + 2 + c) for i in range(first, stop) for c in (0, 1)]
        return permute(x, moves)

    def down(x, first, stop):
        moves = [(2 * i + c, 2 * i - 2 + c) for i in range(first, stop) for c in (0, 1)]
        return permute(x, moves)

    def across(x, k):
        return permute(x, [(i, i ^ k) for i in range(doms)], "dom")

    prepared = prepare(tokens, input_gain)
    step_weight_t = step_weight.T

    at = rank.astype(jnp.int32).reshape(1)
    above = [prepared[k] for k in range(CHUNKS)]
    below = list(above)
    hops = [above + [swap(x) for x in above]]
    for s in range(1, pairs):
        for k in range(CHUNKS):
            above[k] = down(above[k], 1, pairs - s + 1)
            below[k] = up(below[k], s - 1, pairs - 1)
        hops.append(
            above + [swap(x) for x in above] + below + [swap(x) for x in below]
        )

    narrow = ()
    for s in range(pairs):
        where = functools.partial(place, s, pairs)
        narrow = project_narrow(
            where, ranks, at, hops[s], mixing_weight, step_weight_t, narrow
        )
    weights = ()
    for s in range(PIECES):
        weights = (split_weights(gate_value_weight, s, weights),)

    history = jnp.concatenate(
        [jnp.moveaxis(value_history, 1, 0), jnp.moveaxis(mixing_history, 1, 0)], axis=2
    ).astype(BF16)
    history, _ = lax.optimization_barrier((history, hops[1][0]))
    history_all = jnp.concatenate([history] + [across(history, k) for k in range(1, doms)], axis=1)
    first_child = dom * particles
    own_parents = lax.dynamic_slice_in_dim(parents, first_child, particles)
    held_at = ((own_parents // particles) ^ dom) * particles + own_parents % particles
    chosen = (held_at[:, None] == jnp.arange(doms * particles)[None, :]).astype(BF16)
    inherited = jnp.einsum("cp,tpw->tcw", chosen, history_all, preferred_element_type=F32)

    per_group = ranks // GROUPS
    group = rank // per_group
    columns = mixing_weight.shape[1]
    shape = (CHUNKS, steps, each)

    mix_raw, step_raw, extra, features_all = narrow
    value_all = project_wide(1, features_all, weights[0])
    gate_all = project_wide(0, features_all, weights[0])
    squares = (extra[:, 0] + extra[:, 1])[:, :rows].reshape(*shape, 1)
    rs = lax.rsqrt(squares / features + 1e-05)
    mixing = jnp.stack(
        [
            conv(
                inherited[:, k * each : (k + 1) * each, channels:],
                mix_raw[k].reshape(steps, each, columns) * rs[k],
                mixing_kernel,
                mixing_offset,
            ).astype(BF16)
            for k in range(CHUNKS)
        ]
    )
    if columns == state_width and per_group == 2:
        moves = [(g, 2 * g) for g in range(GROUPS)]
        moves += [(GROUPS + g, 2 * g + 1) for g in range(GROUPS)]
        mine = permute(mixing, moves)
        other = swap(mine)
        b_all = jnp.where(core == 0, mine, other)
        c_all = jnp.where(core == 0, other, mine)
    else:
        every = lax.all_gather(mixing, "head", axis=3, tiled=True)
        b_all = lax.dynamic_slice_in_dim(every, group * state_width, state_width, 3)
        c_all = lax.dynamic_slice_in_dim(every, (GROUPS + group) * state_width, state_width, 3)
    size_all = jax.nn.softplus(step_raw.reshape(*shape, heads) * rs + step_offset)
    decay_all = jnp.exp(-size_all * jnp.exp(decay_log))

    c_child = jnp.swapaxes(c_all, 1, 2)
    slabs = [c_child] + [across(c_child, j) for j in range(1, doms)]
    stacked = jnp.stack(slabs)
    by_dom = jnp.stack(
        [lax.dynamic_index_in_dim(stacked, dom ^ d, 0, False) for d in range(doms)]
    )

    child_mix = by_dom.reshape(doms * particles, steps, state_width)
    child_mix = jnp.pad(child_mix, ((0, TOGETHER), (0, 0), (0, 0)))
    local = parents - first_child
    held = jnp.arange(particles)[:, None]
    low = jnp.sum((local[None, :] < held).astype(jnp.int32), axis=1)
    high = jnp.sum((local[None, :] <= held).astype(jnp.int32), axis=1)
    state_reads = owner_reads(low, high, child_mix, recurrent_state)
    state_reads = state_reads.reshape(doms, CHUNKS, each, steps, channels)

    def read_states(k):
        holder = lax.dynamic_slice_in_dim(own_parents, k * each, each) // particles
        parts = [
            lax.dynamic_index_in_dim(state_reads[:, k], dom ^ j, 0, False) for j in range(doms)
        ]
        result = parts[0]
        for j in range(1, doms):
            received = across(parts[j], j)
            result = jnp.where((holder == (dom ^ j))[:, None, None], received, result)
        return jnp.moveaxis(result, 1, 0)


    def finish(k, inherited_reads):
        part = slice(k * each, (k + 1) * each)
        y, cumulative = local_reads(
            value_all[k].reshape(steps, each, channels),
            jnp.broadcast_to(rs[k], (steps, each, LANES)),
            inherited[:, part, :channels],
            value_kernel,
            value_offset.reshape(1, -1),
            b_all[k],
            c_all[k],
            pad_lanes(size_all[k].reshape(rows, heads)),
            pad_lanes(decay_all[k].reshape(rows, heads)),
            jnp.broadcast_to(pad_lanes(skip_gain.reshape(1, -1)), (8, LANES)),
            head_width,
        )
        read = cumulative * inherited_reads.astype(F32) + y
        gated = read * silu(gate_all[k].reshape(steps, each, channels) * rs[k])
        squares = jnp.sum(gated * gated, axis=2)
        total = squares
        for r in range(1, per_group):
            turn = [(i, i - i % per_group + (i + r) % per_group) for i in range(ranks)]
            total = total + permute(squares, turn)
        square_mean = total / (per_group * channels)
        return (
            (gated * lax.rsqrt(square_mean + 1e-05)[..., None] * output_gain)
            .reshape(rows, channels)
            .astype(BF16)
        )

    def scatter(scaled):
        blocks = jnp.arange(pairs, dtype=jnp.int32) * 2
        away = project_out(blocks + 1 - core, scaled, output_weight, width)
        here = project_out(blocks + core, scaled, output_weight, width)
        both = here.astype(F32) + swap(away).astype(F32)
        both = both.astype(BF16)

        both_up = lax.optimization_barrier(both)

        def block(d, sums=both):
            return lax.dynamic_index_in_dim(sums, jnp.clip(d, 0, pairs - 1), 0, False).astype(F32)

        above = below = None
        for s in range(1, pairs):
            to_down = block(z - (pairs - s))
            to_up = block(z + (pairs - s), both_up)
            if s > 1:
                to_down, to_up = to_down + above.astype(F32), to_up + below.astype(F32)
            above = down(to_down.astype(BF16), pairs - s, pairs)
            below = up(to_up.astype(BF16), 0, s)
        result = block(z) + above.astype(F32) + below.astype(F32)
        return result.astype(BF16).reshape(steps, each, width)

    reads = [read_states(k) for k in range(CHUNKS)]
    outputs, scaled = [], ()
    for k in range(CHUNKS):
        inherited_reads, _ = lax.optimization_barrier((reads[k], scaled))
        scaled = finish(k, inherited_reads)
        outputs.append(scatter(scaled))
    return jnp.concatenate(outputs, axis=1)


def solution(mesh):
    return jax.shard_map(
        body,
        mesh=mesh,
        in_specs=(
            P(None, "dom", "head"),
            P(),
            P("dom", "head", None, None),
            P("dom", None, "head"),
            P("dom", None, "head"),
            P("head"),
            P(None, None, "head"),
            P(None, "head"),
            P(None, "head"),
            P(None, "head"),
            P("head"),
            P(None, "head"),
            P("head"),
            P("head"),
            P("head"),
            P("head"),
            P("head"),
            P("head", None),
        ),
        out_specs=P(None, "dom", "head"),
        check_vma=False,
    )
```
